128 devices in a mesh: depth: 2 (over core), row: 2 (over x_hi), col: 32 (over z, y, x_lo).
Axes of the slice: x: 4 (x_hi: 2, x_lo: 2; x = x_hi * 2 + x_lo), y: 4, z: 4, core: 2. Of those that a mesh axis runs over, the one named last changes fastest.
Arguments:
- probe: float32 [2, 256, 256], replicated, may hold values from -6 to 6
- object_re: bfloat16 [2, 1024, 32768], P('depth', 'row', 'col'), may hold values from 0.099609375 to 1.8984375
- object_im: bfloat16 [2, 1024, 32768], P('depth', 'row', 'col'), may hold values from -1.796875 to 1.796875
- phases: float32 [256, 256], replicated, may hold values from -3.140625 to 3.140625
- centres: int32 [2, 32, 4, 2, 2], P('row', 'col'), may hold values from 0 to 1023, as said below
- occupied: int32 [2, 32, 4], P('row', 'col'), may hold values from 0 to 2, as said below
- measured: float32 [2, 32, 4, 2, 256, 256], P('row', 'col'), may hold values from 0 to 4
Outputs:
- object_grad: float32 [2, 2, 1024, 32768], P(None, 'depth', 'row', 'col')
- probe_grad: float32 [2, 256, 256], P(None, 'depth')
The draws below stay inside these ranges and needn't reach their ends.
Inputs may be any that keep to these rules, and one draw needn't show every extreme that they name: `centres`: the 256 x 256 window around every centre, starting 256 // 2 pixels before it in both directions, lies inside the field of view. `occupied`: in every draw some tile has all 2 slots used in some micro-batch.
All inputs are finite; a program needn't handle non-finite values.
Results may differ from the reference program's by a relative error of at most 0.006.
Values may be sent and summed in bfloat16 or wider, within the bound.
A program may use at most 192 MiB of HBM per device.

```python
import jax
import jax.numpy as jnp
from jax import lax

P_SIZE = 256
TR = 512
TC = 1024
MB = 4
CAP = 2
SLICES = 2
GRID_R = 2
GRID_C = 32
NY = 1024
NX = 32768


def draw_centres(key, part):
    half_size = P_SIZE // 2
    grid_shape = (GRID_R, GRID_C, MB, CAP)
    row_ids = jnp.arange(GRID_R, dtype=jnp.int32).reshape(GRID_R, 1, 1, 1)
    col_ids = jnp.arange(GRID_C, dtype=jnp.int32).reshape(1, GRID_C, 1, 1)
    low_rows = jnp.broadcast_to(jnp.where(row_ids == 0, half_size, 0), grid_shape)
    high_rows = jnp.broadcast_to(jnp.where(row_ids == GRID_R - 1, TR - half_size, TR), grid_shape)
    low_cols = jnp.broadcast_to(jnp.where(col_ids == 0, half_size, 0), grid_shape)
    high_cols = jnp.broadcast_to(jnp.where(col_ids == GRID_C - 1, TC - half_size, TC), grid_shape)
    key_rows, key_cols = jax.random.split(jax.random.fold_in(key, 11))
    centre_rows = jax.random.randint(key_rows, grid_shape, low_rows, high_rows, dtype=jnp.int32)
    centre_cols = jax.random.randint(key_cols, grid_shape, low_cols, high_cols, dtype=jnp.int32)
    return jnp.stack([centre_rows, centre_cols], axis=-1)


def draw_occupied(key, part):
    key_counts, key_pick = jax.random.split(jax.random.fold_in(key, 23))
    counts = jax.random.randint(key_counts, (GRID_R, GRID_C, MB), 0, CAP + 1, dtype=jnp.int32)
    chosen = jax.random.randint(key_pick, (), 0, GRID_R * GRID_C * MB, dtype=jnp.int32)
    flattened = counts.reshape(-1)
    positions = jnp.arange(GRID_R * GRID_C * MB, dtype=jnp.int32)
    flattened = jnp.where(positions == chosen, CAP, flattened)
    return flattened.reshape(GRID_R, GRID_C, MB)


def steps_of(own_key, shape, pieces, least, high):
    def one(dim, blocks):
        steps = jax.random.uniform(jax.random.fold_in(jax.random.fold_in(own_key, 6), dim), (blocks,), jnp.float32, least / len(pieces), high / len(pieces))
        return jnp.repeat(jnp.exp(steps), shape[dim] // blocks).reshape((-1,) + (1,) * (len(shape) - dim - 1))

    loudness = one(*pieces[0])
    for cut in pieces[1:]:
        loudness = loudness * one(*cut)
    return loudness


def noise(own_key, shape, scale, reach, pieces=(), kind=jnp.bfloat16):
    level = steps_of(own_key, shape, pieces, -0.22, 0.18) if pieces else 1.0
    result = jax.random.normal(own_key, shape, jnp.float32) * scale * level
    return jnp.minimum(jnp.maximum(result, -reach), reach).astype(kind)


def setup_inputs(seed: int = 0) -> dict:
    streams_of = jax.random.split(jax.random.key(seed), 8)
    return {
        "probe": noise(streams_of[0], (2, P_SIZE, P_SIZE), 1.0, 6.0, (), jnp.float32),
        "object_re": jnp.clip(1.0 + 0.18 * jax.random.normal(streams_of[1], (SLICES, NY, NX), jnp.float32), 0.099609375, 1.8984375).astype(jnp.bfloat16),
        "object_im": noise(streams_of[2], (SLICES, NY, NX), 0.3, 1.796875, ((0, 2), (1, 2), (2, 32))),
        "phases": jnp.clip(jax.random.uniform(streams_of[3], (P_SIZE, P_SIZE), jnp.float32, -3.140625, 3.140625), -3.140625, 3.140625),
        "centres": draw_centres(jax.random.fold_in(streams_of[7], 71), 0),
        "occupied": draw_occupied(jax.random.fold_in(streams_of[7], 71), 0),
        "measured": jnp.clip(4.0 * jax.random.uniform(streams_of[6], (GRID_R, GRID_C, MB, CAP, P_SIZE, P_SIZE), jnp.float32) ** steps_of(streams_of[6], (GRID_R, GRID_C, MB, CAP, P_SIZE, P_SIZE), ((0, 2), (1, 32)), -0.2, 0.2), 0.0, 4.0),
    }


def rounded(value):
    return lax.optimization_barrier(value.astype(jnp.bfloat16)).astype(value.dtype)


def keep_bf16(value):
    return lax.complex(rounded(jnp.real(value)), rounded(jnp.imag(value)))


def forward_ft(value):
    return jnp.fft.fft2(value, norm="ortho")


def inverse_ft(value):
    return jnp.fft.ifft2(value, norm="ortho")


def reference(probe, object_re, object_im, phases, centres, occupied, measured):
    half_size = P_SIZE // 2
    object_c = lax.complex(object_re.astype(jnp.float32), object_im.astype(jnp.float32))
    kernel = lax.complex(jnp.cos(phases), jnp.sin(phases))
    launch = lax.complex(probe[0], probe[1])
    row_base = (jnp.arange(GRID_R, dtype=jnp.int32) * TR)[:, None, None, None]
    col_base = (jnp.arange(GRID_C, dtype=jnp.int32) * TC)[None, :, None, None]
    top_row = (centres[..., 0] + row_base - half_size).astype(jnp.int32).reshape(-1)
    left_col = (centres[..., 1] + col_base - half_size).astype(jnp.int32).reshape(-1)
    slot_ids = jnp.arange(CAP, dtype=jnp.int32)[None, None, None, :]
    live_all = (slot_ids < occupied[..., None]).astype(jnp.float32).reshape(-1)
    frames = measured.reshape(-1, P_SIZE, P_SIZE)

    def visit_one(carry, record):
        gradient, probe_sum = carry
        top_px, left_px, live_w, measure = record
        windows = []
        for slice_no in range(SLICES):
            anchor = (jnp.asarray(slice_no, jnp.int32), top_px, left_px)
            windows.append(lax.dynamic_slice(object_c, anchor, (1, P_SIZE, P_SIZE))[0])
        incident = [launch]
        for slice_no in range(SLICES - 1):
            incident.append(keep_bf16(inverse_ft(kernel * forward_ft(incident[slice_no] * windows[slice_no]))))
        farfield = forward_ft(incident[-1] * windows[-1])
        misfit = jnp.real(farfield) ** 2 + jnp.imag(farfield) ** 2 - measure
        adjoint = inverse_ft(misfit * farfield)
        for slice_no in range(SLICES - 1, -1, -1):
            anchor = (jnp.asarray(slice_no, jnp.int32), top_px, left_px)
            contrib = live_w * jnp.conj(incident[slice_no]) * adjoint
            previous = lax.dynamic_slice(gradient, anchor, (1, P_SIZE, P_SIZE))
            gradient = lax.dynamic_update_slice(gradient, previous + contrib[None], anchor)
            pulled = jnp.conj(windows[slice_no]) * adjoint
            if slice_no > 0:
                adjoint = keep_bf16(inverse_ft(jnp.conj(kernel) * forward_ft(pulled)))
            else:
                probe_sum = probe_sum + live_w * pulled
        return (gradient, probe_sum), None

    start = (jnp.zeros(object_c.shape, object_c.dtype), jnp.zeros(launch.shape, launch.dtype))
    (gradient, probe_sum), _ = lax.scan(visit_one, start, (top_row, left_col, live_all, frames))
    object_grad = jnp.stack([jnp.real(gradient), jnp.imag(gradient)])
    probe_grad = jnp.stack([jnp.real(probe_sum), jnp.imag(probe_sum)])
    return object_grad, probe_grad
```

```python
import functools

import jax
import jax.numpy as jnp
import numpy as np
from jax import lax
from jax.experimental import pallas as pl
from jax.experimental.pallas import tpu as pltpu
from jax.sharding import PartitionSpec as P

MESH = pl.DeviceIdType.MESH
F32 = jnp.float32
BF16 = jnp.bfloat16
ANY = pl.BlockSpec(memory_space=pl.ANY)
LANE = 128


def constants(n):
    half = n // 2
    k = np.arange(half)
    parts = []
    for parity in range(2):
        turns = (np.outer(2 * k + parity, k) % n) / n
        w = np.exp(-2j * np.pi * turns) / np.sqrt(n)
        block = np.block([[w.real, -w.imag], [w.imag, w.real]])
        for matrix in (block, block.T):
            high = matrix.astype(np.float32).astype(BF16)
            low = (matrix - high.astype(np.float64)).astype(np.float32).astype(BF16)
            parts += [high, low]
    order = np.concatenate([np.arange(0, n, 2), np.arange(1, n, 2)])
    perm = np.zeros((n, n), np.float32)
    perm[np.arange(n), order] = 1.0
    return np.stack(parts), np.stack([perm, perm.T]).astype(BF16)


def axis_ids():
    return lax.axis_index("depth"), lax.axis_index("row"), lax.axis_index("col")


def meet(peers):
    barrier = pltpu.get_barrier_semaphore()
    for peer in peers:
        pl.semaphore_signal(barrier, inc=1, device_id=peer, device_id_type=MESH)
    pl.semaphore_wait(barrier, len(peers))


def remote(src, dst, sems, slot, peer):
    return pltpu.make_async_remote_copy(
        src_ref=src, dst_ref=dst, send_sem=sems[0].at[slot], recv_sem=sems[1].at[slot], device_id=peer, device_id_type=MESH
    )


def neighbours():
    d, r, c = axis_ids()
    cols = lax.axis_size("col")
    right, left = lax.rem(c + 1, cols), lax.rem(c + cols - 1, cols)
    return [(d, 1 - r, c), (d, r, right), (d, r, left), (d, 1 - r, right), (d, 1 - r, left)]


def halo_kernel(rows, cols, halo, re_ref, im_ref, out_ref, stage, send, recv, own):
    _, r, _ = axis_ids()
    peers = neighbours()
    loads = [pltpu.make_async_copy(src.at[0], stage.at[p], own.at[p]) for p, src in enumerate((re_ref, im_ref))]
    for load in loads:
        load.start()
    meet(peers)
    edge = pl.ds(pl.multiple_of((rows - halo) * (1 - r), halo), halo)
    far = pl.ds(pl.multiple_of(rows * r, halo), halo)
    mine = pl.ds(pl.multiple_of(halo * r, halo), rows)
    everything, first, last = pl.ds(0, rows), pl.ds(0, halo), pl.ds(cols - halo, halo)
    middle, before, after = pl.ds(halo, cols), pl.ds(0, halo), pl.ds(halo + cols, halo)
    moves = [
        (edge, pl.ds(0, cols), far, middle),
        (everything, last, mine, before),
        (everything, first, mine, after),
        (edge, last, far, before),
        (edge, first, far, after),
    ]
    copies = []
    for p, src in enumerate((re_ref, im_ref)):
        for i, (sr, sc, dr, dc) in enumerate(moves):
            copies.append(remote(src.at[0, sr, sc], out_ref.at[p, dr, dc], (send, recv), p * 5 + i, peers[i]))
    for copy in copies:
        copy.start()
    stores = [pltpu.make_async_copy(stage.at[p], out_ref.at[p, mine, middle], own.at[2 + p]) for p in range(2)]
    for load, store in zip(loads, stores):
        load.wait()
        store.start()
    for store in stores:
        store.wait()
    for copy in copies:
        copy.wait()


def exchange_halo(object_re, object_im, halo):
    _, rows, cols = object_re.shape
    return pl.pallas_call(
        functools.partial(halo_kernel, rows, cols, halo),
        out_shape=jax.ShapeDtypeStruct((2, rows + halo, cols + 2 * halo), object_re.dtype),
        in_specs=[ANY, ANY],
        out_specs=ANY,
        scratch_shapes=[
            pltpu.VMEM((2, rows, cols), object_re.dtype),
            pltpu.SemaphoreType.DMA((10,)),
            pltpu.SemaphoreType.DMA((10,)),
            pltpu.SemaphoreType.DMA((4,)),
        ],
        compiler_params=pltpu.CompilerParams(collective_id=0, has_side_effects=True),
        name="halo_in",
    )(object_re, object_im)


def shifted_in(x, down, right):
    rows, cols = x.shape
    turned = pltpu.roll(x.reshape(rows // 8, 8, cols), jnp.bitwise_and(8 - down, 7), 1)
    sub = lax.broadcasted_iota(jnp.int32, (rows // 8 - 1, 8, cols), 1)
    x = jnp.where(sub < 8 - down, turned[:-1], turned[1:]).reshape(rows - 8, cols)
    turned = [pltpu.roll(x[:, i : i + LANE], jnp.bitwise_and(LANE - right, LANE - 1), 1) for i in range(0, cols, LANE)]
    lanes = lax.broadcasted_iota(jnp.int32, turned[0].shape, 1)
    return jnp.concatenate([jnp.where(lanes < LANE - right, a, b) for a, b in zip(turned[:-1], turned[1:])], 1)


def shifted_out(x, down, right):
    rows, cols = x.shape
    turned = [pltpu.roll(x[:, i : i + LANE], right, 1) for i in range(0, cols, LANE)]
    lanes = lax.broadcasted_iota(jnp.int32, turned[0].shape, 1)
    none = jnp.zeros_like(turned[0])
    x = jnp.concatenate([jnp.where(lanes < right, a, b) for a, b in zip([none] + turned, turned + [none])], 1)
    cols = cols + LANE
    turned = pltpu.roll(x.reshape(rows // 8, 8, cols), down, 1)
    none = jnp.zeros((1, 8, cols), x.dtype)
    sub = lax.broadcasted_iota(jnp.int32, (rows // 8 + 1, 8, cols), 1)
    both = jnp.where(sub < down, jnp.concatenate([none, turned], 0), jnp.concatenate([turned, none], 0))
    return both.reshape(rows + 8, cols)


def extract_kernel(n, rows_all, at_ref, pad_ref, mine_ref, theirs_ref, wide):
    k = pl.program_id(0)
    row, col = at_ref[k, 0], at_ref[k, 1]
    tall = n + 16
    base = pl.multiple_of(jnp.minimum(row // 16 * 16, rows_all - tall), 16)
    lane = pl.multiple_of(col // LANE * LANE, LANE)
    down, right = row - base, col - lane
    skip = pl.multiple_of(down // 8 * 8, 8)
    down = down - skip
    for p in range(2):
        wide[pl.ds(0, tall), :] = pad_ref[p, pl.ds(base, tall), pl.ds(lane, n + LANE)].astype(F32)
        window = shifted_in(wide[pl.ds(skip, n + 8), :], down, right).astype(BF16)
        @pl.when(k < 4)
        def _():
            mine_ref[0, p] = window
        @pl.when(k >= 4)
        def _():
            theirs_ref[0, p] = window


def extract(starts, padded, n):
    count = starts.shape[0]
    half = count // 2
    rows_all, cols_all = padded.shape[1:]
    shape = jax.ShapeDtypeStruct((half, 2, n, n), BF16)
    return pl.pallas_call(
        functools.partial(extract_kernel, n, rows_all),
        out_shape=(shape, shape),
        grid_spec=pltpu.PrefetchScalarGridSpec(
            num_scalar_prefetch=1,
            grid=(count,),
            in_specs=[pl.BlockSpec((2, rows_all, cols_all), lambda k, at: (0, 0, 0), pipeline_mode=pl.Buffered(1))],
            out_specs=(
                pl.BlockSpec((1, 2, n, n), lambda k, at: (jnp.minimum(k, half - 1), 0, 0, 0)),
                pl.BlockSpec((1, 2, n, n), lambda k, at: (jnp.maximum(k - half, 0), 0, 0, 0)),
            ),
            scratch_shapes=[pltpu.VMEM((n + 24, n + LANE), F32)],
        ),
        name="extract",
    )(starts, padded)


def swap_kernel(count, *refs):
    d, r, c = axis_ids()
    peer = (1 - d, r, c)
    sources, targets, (send, recv) = refs[:count], refs[count : 2 * count], refs[2 * count :]
    meet([peer])
    copies = [remote(s, t, (send, recv), i, peer) for i, (s, t) in enumerate(zip(sources, targets))]
    for copy in copies:
        copy.start()
    for copy in copies:
        copy.wait()


def swap(arrays, collective_id, name):
    count = len(arrays)
    return pl.pallas_call(
        functools.partial(swap_kernel, count),
        out_shape=tuple(jax.ShapeDtypeStruct(a.shape, a.dtype) for a in arrays),
        in_specs=[ANY] * count,
        out_specs=tuple([ANY] * count),
        scratch_shapes=[pltpu.SemaphoreType.DMA((count,)), pltpu.SemaphoreType.DMA((count,))],
        compiler_params=pltpu.CompilerParams(collective_id=collective_id, has_side_effects=True),
        name=name,
    )(*arrays)


def split(x):
    high = x.astype(BF16)
    return high, (x - high.astype(F32)).astype(BF16)


def product(a, b, passes):
    (ah, al), (bh, bl) = a, b
    if passes == 3:
        lhs, rhs = [ah, ah, al], [bh, bl, bh]
    else:
        lhs, rhs = [ah], [bh]
    lhs = jnp.concatenate(lhs, 1) if len(lhs) > 1 else lhs[0]
    rhs = jnp.concatenate(rhs, 0) if len(rhs) > 1 else rhs[0]
    return jnp.dot(lhs, rhs, preferred_element_type=F32)


def make_transforms(mats_ref):
    def mat(parity, transposed):
        at = parity * 4 + transposed * 2
        return mats_ref[at], mats_ref[at + 1]

    def forward(zr, zi):
        h = zr.shape[0] // 2
        outs = []
        for parity in range(2):
            fold = (lambda z: z[:h] + z[h:]) if parity == 0 else (lambda z: z[:h] - z[h:])
            outs.append(product(mat(parity, 0), split(jnp.concatenate([fold(zr), fold(zi)], 0)), 3))
        yr = jnp.concatenate([outs[0][:h], outs[1][:h]], 0)
        yi = jnp.concatenate([outs[0][h:], outs[1][h:]], 0)
        outs = []
        for parity in range(2):
            fold = (lambda z: z[:, :h] + z[:, h:]) if parity == 0 else (lambda z: z[:, :h] - z[:, h:])
            outs.append(product(split(jnp.concatenate([fold(yr), fold(yi)], 1)), mat(parity, 1), 3))
        return (
            jnp.concatenate([outs[0][:, :h], outs[1][:, :h]], 1),
            jnp.concatenate([outs[0][:, h:], outs[1][:, h:]], 1),
        )

    def inverse(zr, zi):
        h = zr.shape[0] // 2
        e = product(mat(0, 1), split(jnp.concatenate([zr[:h], zi[:h]], 0)), 3)
        o = product(mat(1, 1), split(jnp.concatenate([zr[h:], zi[h:]], 0)), 3)
        yr = jnp.concatenate([e[:h] + o[:h], e[:h] - o[:h]], 0)
        yi = jnp.concatenate([e[h:] + o[h:], e[h:] - o[h:]], 0)
        e = product(split(jnp.concatenate([yr[:, :h], yi[:, :h]], 1)), mat(0, 0), 3)
        o = product(split(jnp.concatenate([yr[:, h:], yi[:, h:]], 1)), mat(1, 0), 3)
        return (
            jnp.concatenate([e[:, :h] + o[:, :h], e[:, :h] - o[:, :h]], 1),
            jnp.concatenate([e[:, h:] + o[:, h:], e[:, h:] - o[:, h:]], 1),
        )

    return forward, inverse


def cmul(ar, ai, br, bi):
    return ar * br - ai * bi, ar * bi + ai * br


def conj_mul(ar, ai, br, bi):
    return ar * br + ai * bi, ar * bi - ai * br


def rounded(x):
    return x.astype(BF16).astype(F32)


def wave_kernel(half, info_ref, probe_ref, phases_ref, mats_ref, perm_ref, mine_ref, other_ref, frame_ref, grads_ref, keep_ref, give_ref, kern, total):
    k = pl.program_id(0)
    d = info_ref[0]
    forward, inverse = make_transforms(mats_ref)

    def reorder(x, rows):
        high, low = split(x)
        if rows:
            high = jnp.dot(perm_ref[0], high, preferred_element_type=F32).astype(BF16)
            low = jnp.dot(perm_ref[0], low, preferred_element_type=F32).astype(BF16)
        return jnp.dot(high, perm_ref[1], preferred_element_type=F32) + jnp.dot(low, perm_ref[1], preferred_element_type=F32)

    @pl.when(k == 0)
    def _():
        kern[0] = reorder(jnp.cos(phases_ref[...]), True)
        kern[1] = reorder(jnp.sin(phases_ref[...]), True)
        total[...] = jnp.zeros_like(total)

    live = info_ref[1 + k].astype(F32)
    first = d == 0

    def window(s):
        pick = first if s == 0 else jnp.logical_not(first)
        return [jnp.where(pick, mine_ref[0, p], other_ref[0, p]).astype(F32) for p in range(2)]

    w0r, w0i = window(0)
    fr, fi = forward(*cmul(probe_ref[0], probe_ref[1], w0r, w0i))
    pr, pi = inverse(*cmul(fr, fi, kern[0], kern[1]))
    pr, pi = rounded(pr), rounded(pi)
    w1r, w1i = window(1)
    fr, fi = forward(*cmul(pr, pi, w1r, w1i))
    misfit = fr * fr + fi * fi - reorder(frame_ref[0], True)
    xr, xi = inverse(misfit * fr, misfit * fi)
    gr, gi = conj_mul(pr, pi, xr, xi)
    grads_ref[1, 0, 0] = (gr * live).astype(BF16)
    grads_ref[1, 0, 1] = (gi * live).astype(BF16)
    fr, fi = forward(*conj_mul(w1r, w1i, xr, xi))
    xr, xi = inverse(*conj_mul(kern[0], kern[1], fr, fi))
    xr, xi = rounded(xr), rounded(xi)
    gr, gi = conj_mul(probe_ref[0], probe_ref[1], xr, xi)
    grads_ref[0, 0, 0] = (gr * live).astype(BF16)
    grads_ref[0, 0, 1] = (gi * live).astype(BF16)
    w0r, w0i = window(0)
    lr, li = conj_mul(w0r, w0i, xr, xi)
    total[0] += lr * live
    total[1] += li * live

    @pl.when(k == half - 1)
    def _():
        n = total.shape[1]
        h = n // 2
        for p in range(2):
            keep_ref[p] = jnp.where(first, total[p, :h], total[p, h:])
            give_ref[p] = jnp.where(first, total[p, h:], total[p, :h]).astype(BF16)


def waves(info, probe, phases, mine, other, frames):
    half, _, n, _ = mine.shape
    mats, perm = constants(n)
    fixed = lambda shape: pl.BlockSpec(shape, lambda k, i: (0,) * len(shape), pipeline_mode=pl.Buffered(1))
    window = pl.BlockSpec((1, 2, n, n), lambda k, i: (k, 0, 0, 0))
    return pl.pallas_call(
        functools.partial(wave_kernel, half),
        out_shape=(
            jax.ShapeDtypeStruct((2, half, 2, n, n), BF16),
            jax.ShapeDtypeStruct((2, n // 2, n), F32),
            jax.ShapeDtypeStruct((2, n // 2, n), BF16),
        ),
        grid_spec=pltpu.PrefetchScalarGridSpec(
            num_scalar_prefetch=1,
            grid=(half,),
            in_specs=[
                fixed((2, n, n)),
                fixed((n, n)),
                fixed(mats.shape),
                fixed(perm.shape),
                window,
                window,
                pl.BlockSpec((1, n, n), lambda k, i: (i[0] * half + k, 0, 0)),
            ],
            out_specs=(
                pl.BlockSpec((2, 1, 2, n, n), lambda k, i: (0, k, 0, 0, 0)),
                pl.BlockSpec((2, n // 2, n), lambda k, i: (0, 0, 0)),
                pl.BlockSpec((2, n // 2, n), lambda k, i: (0, 0, 0)),
            ),
            scratch_shapes=[pltpu.VMEM((2, n, n), F32), pltpu.VMEM((2, n, n), F32)],
        ),
        name="waves",
    )(info, probe, phases, jnp.asarray(mats), jnp.asarray(perm), mine, other, frames)


def scatter_kernel(half, rows, cols, halo, at_ref, mine_ref, got_ref, centre_ref, row_ref, side_ref, corner_ref, acc):
    k = pl.program_id(0)
    n = mine_ref.shape[-1]

    @pl.when(k == 0)
    def _():
        acc[...] = jnp.zeros_like(acc)

    row, col = at_ref[k, 0], at_ref[k, 1]
    lane = pl.multiple_of(col // LANE * LANE, LANE)
    top = pl.multiple_of(row // 8 * 8, 8)
    for p in range(2):
        x = jnp.where(k < half, mine_ref[0, 0, p], got_ref[0, p]).astype(F32)
        acc[p, pl.ds(top, n + 8), pl.ds(lane, n + LANE)] += shifted_out(x, row - top, col - lane)

    @pl.when(k == 2 * half - 1)
    def _():
        up = at_ref[2 * half, 0]
        mine = pl.ds(pl.multiple_of(halo * up, halo), rows)
        far = pl.ds(pl.multiple_of(rows * (1 - up), halo), halo)
        for p in range(2):
            centre_ref[p] = acc[p, mine, pl.ds(halo, cols)]
            row_ref[p] = acc[p, far, pl.ds(halo, cols)].astype(BF16)
            for i, at in enumerate((halo + cols, 0)):
                side_ref[i, p] = acc[p, mine, pl.ds(at, halo)].astype(BF16)
                corner_ref[i, p] = acc[p, far, pl.ds(at, halo)].astype(BF16)


def scatter(places, grads, got, rows, cols, halo):
    half, _, n, _ = got.shape
    full = lambda shape: pl.BlockSpec(shape, lambda k, i: (0,) * len(shape))
    shapes = [((2, rows, cols), F32), ((2, halo, cols), BF16), ((2, 2, rows, halo), BF16), ((2, 2, halo, halo), BF16)]
    return pl.pallas_call(
        functools.partial(scatter_kernel, half, rows, cols, halo),
        out_shape=tuple(jax.ShapeDtypeStruct(s, t) for s, t in shapes),
        grid_spec=pltpu.PrefetchScalarGridSpec(
            num_scalar_prefetch=1,
            grid=(2 * half,),
            in_specs=[
                pl.BlockSpec((1, 1, 2, n, n), lambda k, i: (i[2 * half, 1], jnp.minimum(k, half - 1), 0, 0, 0)),
                pl.BlockSpec((1, 2, n, n), lambda k, i: (jnp.maximum(k - half, 0), 0, 0, 0)),
            ],
            out_specs=tuple(full(s) for s, _ in shapes),
            scratch_shapes=[pltpu.VMEM((2, rows + halo + 8, cols + 2 * halo), F32)],
        ),
        name="scatter",
    )(places, grads, got)


def x_peer(q):
    d, _, c = axis_ids()
    return (d, q // 2, c // 2 * 2 + lax.rem(q, 2))


def plane_peer(q):
    d, r, c = axis_ids()
    return (d, r, q * 2 + lax.rem(c, 2))


def return_kernel(row_ref, side_ref, corner_ref, keep_ref, got_ref, row_out, side_out, corner_out, probe_out, buf, line, plane, gathered, strips, xs, ps, gs, fs):
    d, r, c = axis_ids()
    planes = lax.axis_size("col") // 2
    my_x = r * 2 + lax.rem(c, 2)
    my_p = c // 2
    peers = neighbours()
    line_peers = [lax.rem(my_x + t, 4) for t in range(1, 4)]
    plane_peers = [lax.rem(my_p + t, planes) for t in range(1, planes)]
    meet(peers + [x_peer(q) for q in line_peers] + [plane_peer(q) for q in plane_peers])
    pairs = [
        (row_ref, row_out, peers[0]),
        (side_ref.at[0], side_out.at[0], peers[1]),
        (side_ref.at[1], side_out.at[1], peers[2]),
        (corner_ref.at[0], corner_out.at[0], peers[3]),
        (corner_ref.at[1], corner_out.at[1], peers[4]),
    ]
    copies = [remote(s, t, strips, i, peer) for i, (s, t, peer) in enumerate(pairs)]
    for copy in copies:
        copy.start()
    half_rows, n = keep_ref.shape[1:]
    at = 0
    for p in range(2):
        for t in range(half_rows // 8):
            for h in range(n // LANE):
                place = (p, pl.ds(8 * t, 8), pl.ds(LANE * h, LANE))
                buf[at] = keep_ref[place] + got_ref[place].astype(F32)
                at += 1
    share = at // 4

    def piece(ref, q):
        return ref.at[pl.ds(q * share, share)]

    sent = []
    for q in line_peers:
        sent.append(pltpu.make_async_remote_copy(piece(buf, q), line.at[my_x], xs[0].at[q], xs[1].at[my_x], device_id=x_peer(q), device_id_type=MESH))
        sent[-1].start()
    for q in line_peers:
        pltpu.make_async_remote_copy(piece(buf, q), line.at[q], xs[0].at[q], xs[1].at[q], device_id=x_peer(q), device_id_type=MESH).wait_recv()
    total = buf[pl.ds(my_x * share, share)]
    for q in line_peers:
        total = total + line[q]
    plane[my_p] = total
    for q in plane_peers:
        sent.append(pltpu.make_async_remote_copy(plane.at[my_p, q], gathered.at[my_p], ps[0].at[q], ps[1].at[my_p], device_id=plane_peer(q), device_id_type=MESH))
        sent[-1].start()
    for q in plane_peers:
        pltpu.make_async_remote_copy(plane.at[my_p, q], gathered.at[q], ps[0].at[q], ps[1].at[q], device_id=plane_peer(q), device_id_type=MESH).wait_recv()
    mine = plane[my_p, my_p]
    for q in plane_peers:
        mine = mine + gathered[q]
    probe_out[my_x * share + my_p] = mine
    own = probe_out.at[my_x * share + my_p]
    for q in plane_peers:
        sent.append(pltpu.make_async_remote_copy(own, own, gs[0].at[q], gs[1].at[my_p], device_id=plane_peer(q), device_id_type=MESH))
        sent[-1].start()
    for q in plane_peers:
        there = probe_out.at[my_x * share + q]
        pltpu.make_async_remote_copy(there, there, gs[0].at[q], gs[1].at[q], device_id=plane_peer(q), device_id_type=MESH).wait_recv()
    for q in line_peers:
        block = piece(probe_out, my_x)
        sent.append(pltpu.make_async_remote_copy(block, block, fs[0].at[q], fs[1].at[my_x], device_id=x_peer(q), device_id_type=MESH))
        sent[-1].start()
    for q in line_peers:
        block = piece(probe_out, q)
        pltpu.make_async_remote_copy(block, block, fs[0].at[q], fs[1].at[q], device_id=x_peer(q), device_id_type=MESH).wait_recv()
    for copy in sent:
        copy.wait_send()
    for copy in copies:
        copy.wait()


def send_back(row, side, corner, keep, got):
    chunks = keep.size // (8 * LANE)
    share = chunks // 4
    vmem = pl.BlockSpec(memory_space=pltpu.VMEM)
    dma = lambda n: [pltpu.SemaphoreType.DMA((n,)), pltpu.SemaphoreType.DMA((n,))]
    return pl.pallas_call(
        return_kernel_flat,
        out_shape=tuple(jax.ShapeDtypeStruct(a.shape, a.dtype) for a in (row, side, corner)) + (jax.ShapeDtypeStruct((chunks, 8, LANE), F32),),
        in_specs=[ANY, ANY, ANY, vmem, vmem],
        out_specs=(ANY, ANY, ANY, vmem),
        scratch_shapes=[
            pltpu.VMEM((chunks, 8, LANE), F32),
            pltpu.VMEM((4, share, 8, LANE), F32),
            pltpu.VMEM((share, share, 8, LANE), F32),
            pltpu.VMEM((share, 8, LANE), F32),
        ]
        + dma(5) + dma(4) + dma(share) + dma(share) + dma(4),
        compiler_params=pltpu.CompilerParams(collective_id=3, has_side_effects=True),
        name="halo_out",
    )(row, side, corner, keep, got)


def return_kernel_flat(*refs):
    sems = refs[13:]
    return_kernel(*refs[:13], *[sems[i : i + 2] for i in range(0, 10, 2)])


def fold_kernel(halo, info_ref, centre_ref, row_ref, side_ref, corner_ref, chunks_ref, out_ref, probe_ref):
    up = info_ref[0]
    _, rows, cols = centre_ref.shape
    edge = pl.ds(pl.multiple_of((rows - halo) * (1 - up), halo), halo)
    out_ref[:, 0] = centre_ref[...]
    for p in range(2):
        out_ref[p, 0, edge, :] += row_ref[p].astype(F32)
        for i, at in enumerate((0, cols - halo)):
            lanes = pl.ds(at, halo)
            out_ref[p, 0, :, lanes] += side_ref[i, p].astype(F32)
            out_ref[p, 0, edge, lanes] += corner_ref[i, p].astype(F32)
    at = 0
    _, half_rows, n = probe_ref.shape
    for p in range(2):
        for t in range(half_rows // 8):
            for h in range(n // LANE):
                probe_ref[p, pl.ds(8 * t, 8), pl.ds(LANE * h, LANE)] = chunks_ref[at]
                at += 1


def fold(info, centre, row, side, corner, chunks, n):
    halo = row.shape[1]
    _, rows, cols = centre.shape
    return pl.pallas_call(
        functools.partial(fold_kernel, halo),
        out_shape=(jax.ShapeDtypeStruct((2, 1, rows, cols), F32), jax.ShapeDtypeStruct((2, n // 2, n), F32)),
        in_specs=[pl.BlockSpec(memory_space=pltpu.SMEM)] + [pl.BlockSpec(memory_space=pltpu.VMEM)] * 5,
        out_specs=(pl.BlockSpec(memory_space=pltpu.VMEM),) * 2,
        name="fold",
    )(info, centre, row, side, corner, chunks)


def shards(probe, object_re, object_im, phases, centres, occupied, measured):
    n = probe.shape[1]
    halo = n // 2
    _, rows, cols = object_re.shape
    batches, slots = centres.shape[2:4]
    count = batches * slots
    half = count // 2
    d, r, _ = axis_ids()
    starts = centres[0, 0].reshape(count, 2) + jnp.stack([halo * (r - 1), jnp.zeros_like(r)])
    starts = jnp.where(d == 0, starts, jnp.concatenate([starts[half:], starts[:half]]))
    live = (jnp.arange(slots, dtype=jnp.int32)[None] < occupied[0, 0][:, None]).reshape(2, half).astype(jnp.int32)
    info = jnp.concatenate([d[None].astype(jnp.int32), jnp.where(d == 0, live[0], live[1])])
    places = jnp.concatenate([starts, jnp.stack([r, d])[None].astype(jnp.int32)])
    padded = exchange_halo(object_re, object_im, halo)
    mine, theirs = extract(starts, padded, n)
    (other,) = swap((theirs,), 1, "swap_in")
    grads, keep, give = waves(info, probe, phases, mine, other, measured[0, 0].reshape(count, n, n))
    away = lax.dynamic_index_in_dim(grads, 1 - d, 0, False)
    got, given = swap((away, give), 2, "swap_out")
    centre, row, side, corner = scatter(places, grads, got, rows, cols, halo)
    row, side, corner, chunks = send_back(row, side, corner, keep, given)
    return fold(r[None].astype(jnp.int32), centre, row, side, corner, chunks, n)


def solution(mesh):
    in_specs = (
        P(),
        P("depth", "row", "col"),
        P("depth", "row", "col"),
        P(),
        P("row", "col", None, None, None),
        P("row", "col", None),
        P("row", "col", None, None, None, None),
    )
    out_specs = (P(None, "depth", "row", "col"), P(None, "depth", None))
    return jax.shard_map(shards, mesh=mesh, in_specs=in_specs, out_specs=out_specs, check_vma=False)
```

```python
import functools

import jax
import jax.numpy as jnp
import numpy as np
from jax import lax
from jax.experimental import pallas as pl
from jax.experimental.pallas import tpu as pltpu
from jax.sharding import PartitionSpec as P

MESH = pl.DeviceIdType.MESH
F32 = jnp.float32
BF16 = jnp.bfloat16
ANY = pl.BlockSpec(memory_space=pl.ANY)
LANE = 128
ORDER = ((), (0, 1), (2,), (3,))
REDUCE = True
NAME = 'halo_out'


def constants(n):
    half = n // 2
    k = np.arange(half)
    parts = []
    for parity in range(2):
        turns = (np.outer(2 * k + parity, k) % n) / n
        w = np.exp(-2j * np.pi * turns) / np.sqrt(n)
        block = np.block([[w.real, -w.imag], [w.imag, w.real]])
        for matrix in (block, block.T):
            high = matrix.astype(np.float32).astype(BF16)
            low = (matrix - high.astype(np.float64)).astype(np.float32).astype(BF16)
            parts += [high, low]
    order = np.concatenate([np.arange(0, n, 2), np.arange(1, n, 2)])
    perm = np.zeros((n, n), np.float32)
    perm[np.arange(n), order] = 1.0
    return np.stack(parts), np.stack([perm, perm.T]).astype(BF16)


def axis_ids():
    return lax.axis_index("depth"), lax.axis_index("row"), lax.axis_index("col")


def meet(peers):
    barrier = pltpu.get_barrier_semaphore()
    for peer in peers:
        pl.semaphore_signal(barrier, inc=1, device_id=peer, device_id_type=MESH)
    pl.semaphore_wait(barrier, len(peers))


def remote(src, dst, sems, slot, peer):
    return pltpu.make_async_remote_copy(
        src_ref=src, dst_ref=dst, send_sem=sems[0].at[slot], recv_sem=sems[1].at[slot], device_id=peer, device_id_type=MESH
    )


def neighbours():
    d, r, c = axis_ids()
    cols = lax.axis_size("col")
    right, left = lax.rem(c + 1, cols), lax.rem(c + cols - 1, cols)
    return [(d, 1 - r, c), (d, r, right), (d, r, left), (d, 1 - r, right), (d, 1 - r, left)]


def shifted_in(x, down, right):
    rows, cols = x.shape
    turned = pltpu.roll(x.reshape(rows // 8, 8, cols), jnp.bitwise_and(8 - down, 7), 1)
    sub = lax.broadcasted_iota(jnp.int32, (rows // 8 - 1, 8, cols), 1)
    x = jnp.where(sub < 8 - down, turned[:-1], turned[1:]).reshape(rows - 8, cols)
    turned = [pltpu.roll(x[:, i : i + LANE], jnp.bitwise_and(LANE - right, LANE - 1), 1) for i in range(0, cols, LANE)]
    lanes = lax.broadcasted_iota(jnp.int32, turned[0].shape, 1)
    return jnp.concatenate([jnp.where(lanes < LANE - right, a, b) for a, b in zip(turned[:-1], turned[1:])], 1)


def shifted_out(x, down, right):
    rows, cols = x.shape
    turned = [pltpu.roll(x[:, i : i + LANE], right, 1) for i in range(0, cols, LANE)]
    lanes = lax.broadcasted_iota(jnp.int32, turned[0].shape, 1)
    none = jnp.zeros_like(turned[0])
    x = jnp.concatenate([jnp.where(lanes < right, a, b) for a, b in zip([none] + turned, turned + [none])], 1)
    cols = cols + LANE
    turned = pltpu.roll(x.reshape(rows // 8, 8, cols), down, 1)
    none = jnp.zeros((1, 8, cols), x.dtype)
    sub = lax.broadcasted_iota(jnp.int32, (rows // 8 + 1, 8, cols), 1)
    both = jnp.where(sub < down, jnp.concatenate([none, turned], 0), jnp.concatenate([turned, none], 0))
    return both.reshape(rows + 8, cols)


def split(x):
    high = x.astype(BF16)
    return high, (x - high.astype(F32)).astype(BF16)


def product(a, b, passes):
    (ah, al), (bh, bl) = a, b
    if passes == 3:
        lhs, rhs = [ah, ah, al], [bh, bl, bh]
    else:
        lhs, rhs = [ah], [bh]
    lhs = jnp.concatenate(lhs, 1) if len(lhs) > 1 else lhs[0]
    rhs = jnp.concatenate(rhs, 0) if len(rhs) > 1 else rhs[0]
    return jnp.dot(lhs, rhs, preferred_element_type=F32)


def make_transforms(mats_ref):
    def mat(parity, transposed):
        at = parity * 4 + transposed * 2
        return mats_ref[at], mats_ref[at + 1]

    def forward(zr, zi):
        h = zr.shape[0] // 2
        outs = []
        for parity in range(2):
            fold = (lambda z: z[:h] + z[h:]) if parity == 0 else (lambda z: z[:h] - z[h:])
            outs.append(product(mat(parity, 0), split(jnp.concatenate([fold(zr), fold(zi)], 0)), 3))
        yr = jnp.concatenate([outs[0][:h], outs[1][:h]], 0)
        yi = jnp.concatenate([outs[0][h:], outs[1][h:]], 0)
        outs = []
        for parity in range(2):
            fold = (lambda z: z[:, :h] + z[:, h:]) if parity == 0 else (lambda z: z[:, :h] - z[:, h:])
            outs.append(product(split(jnp.concatenate([fold(yr), fold(yi)], 1)), mat(parity, 1), 3))
        return (
            jnp.concatenate([outs[0][:, :h], outs[1][:, :h]], 1),
            jnp.concatenate([outs[0][:, h:], outs[1][:, h:]], 1),
        )

    def inverse(zr, zi):
        h = zr.shape[0] // 2
        e = product(mat(0, 1), split(jnp.concatenate([zr[:h], zi[:h]], 0)), 3)
        o = product(mat(1, 1), split(jnp.concatenate([zr[h:], zi[h:]], 0)), 3)
        yr = jnp.concatenate([e[:h] + o[:h], e[:h] - o[:h]], 0)
        yi = jnp.concatenate([e[h:] + o[h:], e[h:] - o[h:]], 0)
        e = product(split(jnp.concatenate([yr[:, :h], yi[:, :h]], 1)), mat(0, 0), 3)
        o = product(split(jnp.concatenate([yr[:, h:], yi[:, h:]], 1)), mat(1, 0), 3)
        return (
            jnp.concatenate([e[:, :h] + o[:, :h], e[:, :h] - o[:, :h]], 1),
            jnp.concatenate([e[:, h:] + o[:, h:], e[:, h:] - o[:, h:]], 1),
        )

    return forward, inverse


def cmul(ar, ai, br, bi):
    return ar * br - ai * bi, ar * bi + ai * br


def conj_mul(ar, ai, br, bi):
    return ar * br + ai * bi, ar * bi - ai * br


def rounded(x):
    return x.astype(BF16).astype(F32)


def halo_kernel(half, halo, phases_ref, perm_ref, re_ref, im_ref, frames_ref, pad_ref, kern_ref, ready_ref, stage, frames, send, recv, own):
    d, r, _ = axis_ids()
    _, rows, cols = re_ref.shape
    slots = frames_ref.shape[3]
    batch = half // slots
    peers = neighbours()
    everything, first, last = pl.ds(0, rows), pl.ds(0, halo), pl.ds(cols - halo, halo)
    middle, before, after = pl.ds(halo, cols), pl.ds(0, halo), pl.ds(halo + cols, halo)
    edge = pl.ds(pl.multiple_of((rows - halo) * (1 - r), halo), halo)
    far = pl.ds(pl.multiple_of(rows * r, halo), halo)
    mine = pl.ds(pl.multiple_of(halo * r, halo), rows)
    loads = [pltpu.make_async_copy(src.at[0], stage.at[p], own.at[p]) for p, src in enumerate((re_ref, im_ref))]
    loads.append(pltpu.make_async_copy(frames_ref.at[0, 0, pl.ds(d * batch, batch)], frames, own.at[4]))
    for load in loads:
        load.start()
    meet(peers)
    moves = [
        (edge, pl.ds(0, cols), far, middle),
        (everything, last, mine, before),
        (everything, first, mine, after),
        (edge, last, far, before),
        (edge, first, far, after),
    ]
    copies = []
    for p, src in enumerate((re_ref, im_ref)):
        for i, (sr, sc, dr, dc) in enumerate(moves):
            copies.append(remote(src.at[0, sr, sc], pad_ref.at[p, dr, dc], (send, recv), p * 5 + i, peers[i]))
            copies[-1].start()
    stores = [pltpu.make_async_copy(stage.at[p], pad_ref.at[p, mine, middle], own.at[2 + p]) for p in range(2)]
    for load, store in zip(loads, stores):
        load.wait()
        store.start()
    kern_ref[0] = reorder(jnp.cos(phases_ref[...]), perm_ref, True)
    kern_ref[1] = reorder(jnp.sin(phases_ref[...]), perm_ref, True)
    loads[2].wait()

    @pl.loop(0, half)
    def _(k):
        ready_ref[k] = reorder(frames[k // slots, lax.rem(k, slots)], perm_ref, True)

    for store in stores:
        store.wait()
    for copy in copies:
        copy.wait()


def exchange_halo(object_re, object_im, phases, perm, measured, halo):
    _, rows, cols = object_re.shape
    batches, slots, n = measured.shape[2:5]
    half = batches * slots // 2
    vmem = pl.BlockSpec(memory_space=pltpu.VMEM)
    dma = pltpu.SemaphoreType.DMA
    return pl.pallas_call(
        functools.partial(halo_kernel, half, halo),
        out_shape=(
            jax.ShapeDtypeStruct((2, rows + halo, cols + 2 * halo), BF16),
            jax.ShapeDtypeStruct((2, n, n), F32),
            jax.ShapeDtypeStruct((half, n, n), F32),
        ),
        in_specs=[vmem, vmem, ANY, ANY, ANY],
        out_specs=(ANY, vmem, vmem),
        scratch_shapes=[
            pltpu.VMEM((2, rows, cols), BF16),
            pltpu.VMEM((half // slots, slots, n, n), F32),
            dma((10,)), dma((10,)), dma((5,)),
        ],
        compiler_params=pltpu.CompilerParams(collective_id=0, has_side_effects=True),
        name="halo_in",
    )(phases, perm, object_re, object_im, measured)


def extract_kernel(halo, centres, occupied, pad_ref, mine_ref, theirs_ref, pieces, wide, load, store, done):
    d, r, _ = axis_ids()
    count = pieces.shape[0]
    half = count // 2
    n = done.shape[-1]
    tall = n + 16
    rows_all = pad_ref.shape[1]
    slots = centres.shape[3]

    def place(k):
        at = jnp.where(k < half, (1 - d) * half + k, d * half + k - half)
        batch, slot = at // slots, lax.rem(at, slots)
        row = centres[0, 0, batch, slot, 0] + halo * (r - 1)
        col = centres[0, 0, batch, slot, 1]
        base = pl.multiple_of(jnp.minimum(row // 16 * 16, rows_all - tall), 16)
        lane = pl.multiple_of(col // LANE * LANE, LANE)
        return base, lane, row - base, col - lane, slot < occupied[0, 0, batch]

    def piece_load(k):
        base, lane, _, _, _ = place(k)
        return pltpu.make_async_copy(pad_ref.at[:, pl.ds(base, tall), pl.ds(lane, n + LANE)], pieces.at[k], load.at[k])

    @pl.loop(0, count)
    def _(k):
        piece_load(k).start()

    def cut(k):
        piece_load(k).wait()
        _, _, down, right, live = place(k)
        skip = pl.multiple_of(down // 8 * 8, 8)
        for p in range(2):
            wide[p, pl.ds(0, tall), :] = pieces[k, p].astype(F32)
            window = shifted_in(wide[p, pl.ds(skip, n + 8), :], down - skip, right)
            done[k, p] = jnp.where(live, window, 0.0).astype(BF16)

    for part, out in enumerate((theirs_ref, mine_ref)):
        @pl.loop(0, half)
        def _(k):
            cut(part * half + k)
            pltpu.make_async_copy(done.at[part * half + k], out.at[k], store.at[part * half + k]).start()

    for part, out in enumerate((theirs_ref, mine_ref)):
        for k in range(half):
            pltpu.make_async_copy(done.at[part * half + k], out.at[k], store.at[part * half + k]).wait()


def extract(centres, occupied, padded, n):
    count = occupied.shape[2] * centres.shape[3]
    half = count // 2
    shape = jax.ShapeDtypeStruct((half, 2, n, n), BF16)
    smem = pl.BlockSpec(memory_space=pltpu.SMEM)
    return pl.pallas_call(
        functools.partial(extract_kernel, n // 2),
        out_shape=(shape, shape),
        in_specs=[smem, smem, ANY],
        out_specs=(ANY, ANY),
        scratch_shapes=[
            pltpu.VMEM((count, 2, n + 16, n + LANE), BF16),
            pltpu.VMEM((2, n + 24, n + LANE), F32),
            pltpu.SemaphoreType.DMA((count,)),
            pltpu.SemaphoreType.DMA((count,)),
            pltpu.VMEM((count, 2, n, n), BF16),
        ],
        name="extract",
    )(centres, occupied, padded)


def reorder(x, perm_ref, both):
    high, low = split(x)
    if both:
        high = jnp.dot(perm_ref[0], high, preferred_element_type=F32).astype(BF16)
        low = jnp.dot(perm_ref[0], low, preferred_element_type=F32).astype(BF16)
    return jnp.dot(high, perm_ref[1], preferred_element_type=F32) + jnp.dot(low, perm_ref[1], preferred_element_type=F32)


def wave_kernel(
    half, probe_ref, kern, mats_ref, mine_ref, theirs_ref, frames_ref,
    terms_ref, keep_ref, given_ref,
    windows, frames, grads, total, give, own_sem, frame_sem, swap_send, swap_recv, term_send, term_recv, term_own, give_send, give_recv,
):
    d, r, c = axis_ids()
    n = probe_ref.shape[1]
    partner = (1 - d, r, c)

    def own_copy(k):
        return pltpu.make_async_copy(mine_ref.at[k], windows.at[d, k], own_sem.at[k])

    def frame_copy(k):
        return pltpu.make_async_copy(frames_ref.at[k], frames.at[k], frame_sem.at[k])

    def window_copy(k):
        return remote(theirs_ref.at[k], windows.at[d, k], (swap_send, swap_recv), k, partner)

    def term_copies(k):
        there = terms_ref.at[d * half + k]
        return (
            remote(grads.at[1 - d, k], there, (term_send, term_recv), k, partner),
            pltpu.make_async_copy(grads.at[d, k], there, term_own.at[k]),
        )

    @pl.loop(0, half)
    def _(k):
        own_copy(k).start()
        frame_copy(k).start()

    meet([partner])

    @pl.loop(0, half)
    def _(k):
        window_copy(k).start()

    total[...] = jnp.zeros_like(total)
    forward, inverse = make_transforms(mats_ref)

    @pl.loop(0, half)
    def _(k):
        def window(s):
            return [windows[s, k, p].astype(F32) for p in range(2)]

        own_copy(k).wait()
        frame_copy(k).wait()
        window_copy(k).wait()
        fr, fi = forward(*cmul(probe_ref[0], probe_ref[1], *window(0)))
        pr, pi = inverse(*cmul(fr, fi, kern[0], kern[1]))
        pr, pi = rounded(pr), rounded(pi)
        w1r, w1i = window(1)
        fr, fi = forward(*cmul(pr, pi, w1r, w1i))
        misfit = fr * fr + fi * fi - frames[k]
        xr, xi = inverse(misfit * fr, misfit * fi)
        gr, gi = conj_mul(pr, pi, xr, xi)
        grads[1, k, 0] = gr.astype(BF16)
        grads[1, k, 1] = gi.astype(BF16)
        fr, fi = forward(*conj_mul(w1r, w1i, xr, xi))
        xr, xi = inverse(*conj_mul(kern[0], kern[1], fr, fi))
        xr, xi = rounded(xr), rounded(xi)
        gr, gi = conj_mul(probe_ref[0], probe_ref[1], xr, xi)
        grads[0, k, 0] = gr.astype(BF16)
        grads[0, k, 1] = gi.astype(BF16)
        lr, li = conj_mul(*window(0), xr, xi)
        total[0] += lr
        total[1] += li
        for copy in term_copies(k):
            copy.start()

    mid = n // 2
    for p in range(2):
        give[p] = total[p, pl.ds(pl.multiple_of((1 - d) * mid, 8), mid), :].astype(BF16)
        keep_ref[p] = total[p, pl.ds(pl.multiple_of(d * mid, 8), mid), :]
    last_copy = pltpu.make_async_remote_copy(give, given_ref, give_send, give_recv, device_id=partner, device_id_type=MESH)
    last_copy.start()

    @pl.loop(0, half)
    def _(k):
        for copy in term_copies(k):
            copy.wait()

    last_copy.wait()


def waves(probe, kern, mats, mine, theirs, frames):
    half, _, n, _ = mine.shape
    vmem = pl.BlockSpec(memory_space=pltpu.VMEM)
    dma = pltpu.SemaphoreType.DMA
    return pl.pallas_call(
        functools.partial(wave_kernel, half),
        out_shape=(
            jax.ShapeDtypeStruct((2 * half, 2, n, n), BF16),
            jax.ShapeDtypeStruct((2, n // 2, n), F32),
            jax.ShapeDtypeStruct((2, n // 2, n), BF16),
        ),
        in_specs=[vmem, vmem, vmem, ANY, ANY, ANY],
        out_specs=(ANY, vmem, ANY),
        scratch_shapes=[
            pltpu.VMEM((2, half, 2, n, n), BF16),
            pltpu.VMEM((half, n, n), F32),
            pltpu.VMEM((2, half, 2, n, n), BF16),
            pltpu.VMEM((2, n, n), F32),
            pltpu.VMEM((2, n // 2, n), BF16),
        ]
        + [dma((half,))] * 7 + [dma(()), dma(())],
        compiler_params=pltpu.CompilerParams(collective_id=1, has_side_effects=True),
        name="waves",
    )(probe, kern, mats, mine, theirs, frames)


def scatter_kernel(halo, centres, terms_ref, centre_ref, row_ref, side_ref, corner_ref, terms, acc, load, store):
    _, r, _ = axis_ids()
    count, _, n, _ = terms.shape
    _, _, rows, cols = centre_ref.shape
    slots = centres.shape[3]

    def term_load(k):
        return pltpu.make_async_copy(terms_ref.at[k], terms.at[k], load.at[k])

    for k in range(count):
        term_load(k).start()
    acc[...] = jnp.zeros_like(acc)

    @pl.loop(0, count)
    def _(k):
        term_load(k).wait()
        row = centres[0, 0, k // slots, lax.rem(k, slots), 0] + halo * (r - 1)
        col = centres[0, 0, k // slots, lax.rem(k, slots), 1]
        top = pl.multiple_of(row // 8 * 8, 8)
        lane = pl.multiple_of(col // LANE * LANE, LANE)
        for p in range(2):
            acc[p, pl.ds(top, n + 8), pl.ds(lane, n + LANE)] += shifted_out(terms[k, p].astype(F32), row - top, col - lane)

    mine = pl.ds(pl.multiple_of(halo * r, halo), rows)
    far = pl.ds(pl.multiple_of(rows * (1 - r), halo), halo)
    stores = [pltpu.make_async_copy(acc.at[p, mine, pl.ds(halo, cols)], centre_ref.at[p, 0], store.at[p]) for p in range(2)]
    for copy in stores:
        copy.start()
    for p in range(2):
        row_ref[p] = acc[p, far, pl.ds(halo, cols)].astype(BF16)
        for i, at in enumerate((halo + cols, 0)):
            side_ref[i, p] = acc[p, mine, pl.ds(at, halo)].astype(BF16)
            corner_ref[i, p] = acc[p, far, pl.ds(at, halo)].astype(BF16)
    for copy in stores:
        copy.wait()


def scatter(centres, terms, rows, cols, halo):
    count, _, n, _ = terms.shape
    vmem = pl.BlockSpec(memory_space=pltpu.VMEM)
    shapes = [((2, 1, rows, cols), F32), ((2, halo, cols), BF16), ((2, 2, rows, halo), BF16), ((2, 2, halo, halo), BF16)]
    return pl.pallas_call(
        functools.partial(scatter_kernel, halo),
        out_shape=tuple(jax.ShapeDtypeStruct(s, t) for s, t in shapes),
        in_specs=[pl.BlockSpec(memory_space=pltpu.SMEM), ANY],
        out_specs=(ANY, vmem, vmem, vmem),
        scratch_shapes=[
            pltpu.VMEM(terms.shape, BF16),
            pltpu.VMEM((2, rows + halo + 8, cols + 2 * halo), F32),
            pltpu.SemaphoreType.DMA((count,)),
            pltpu.SemaphoreType.DMA((2,)),
        ],
        name="scatter",
    )(centres, terms)


def x_peer(q):
    d, _, c = axis_ids()
    return (d, q // 2, c // 2 * 2 + lax.rem(q, 2))


def plane_peer(q):
    d, r, c = axis_ids()
    return (d, r, q * 2 + lax.rem(c, 2))


def return_kernel(row_ref, side_ref, corner_ref, keep_ref, got_ref, row_out, side_out, corner_out, probe_out, buf, line, plane, strips, xs, ps, gs):
    d, r, c = axis_ids()
    planes = lax.axis_size("col") // 2
    my_x = r * 2 + lax.rem(c, 2)
    my_p = c // 2
    peers = neighbours()
    line_peers = [lax.rem(my_x + t, 4) for t in range(1, 4)]
    plane_peers = [lax.rem(my_p + t, planes) for t in range(1, planes)]
    meet(peers + [x_peer(q) for q in line_peers] + [plane_peer(q) for q in plane_peers])
    wide = row_ref.shape[-1] // 2
    groups = [[] for _ in range(4)]
    for p in range(2):
        for i in range(2):
            part = (p, slice(None), pl.ds(i * wide, wide))
            groups[2 * p + i].append((row_ref.at[part], row_out.at[part], peers[0]))
            groups[2 * p + i].append((side_ref.at[i, p], side_out.at[i, p], peers[1 + i]))
            groups[2 * p + i].append((corner_ref.at[i, p], corner_out.at[i, p], peers[3 + i]))
    copies = []

    def launch(chosen):
        for s, t, peer in [m for g in chosen for m in groups[g]]:
            copies.append(remote(s, t, strips, len(copies), peer))
            copies[-1].start()

    half_rows, n = keep_ref.shape[1:]
    at = 0
    for p in range(2):
        for t in range(half_rows // 8):
            for h in range(n // LANE):
                place = (p, pl.ds(8 * t, 8), pl.ds(LANE * h, LANE))
                buf[at] = keep_ref[place] + got_ref[place].astype(F32)
                at += 1
    share = at // planes

    def piece(ref, q):
        return ref.at[pl.ds(q * share, share)]

    def send(src, dst, sems, q, me, peer):
        copy = pltpu.make_async_remote_copy(src, dst, sems[0].at[q], sems[1].at[me], device_id=peer, device_id_type=MESH)
        copy.start()
        sent.append(copy)

    def receive(dst, sems, q, peer):
        pltpu.make_async_remote_copy(dst, dst, sems[0].at[q], sems[1].at[q], device_id=peer, device_id_type=MESH).wait_recv()

    sent = []
    launch(ORDER[0])
    for q in plane_peers:
        send(piece(buf, q), plane.at[my_p], ps, q, my_p, plane_peer(q))
    launch(ORDER[1])
    for q in plane_peers:
        receive(plane.at[q], ps, q, plane_peer(q))
    total = buf[pl.ds(my_p * share, share)]
    for q in plane_peers:
        total = total + plane[q]
    line[my_x] = total
    for q in line_peers:
        send(line.at[my_x], line.at[my_x], xs, q, my_x, x_peer(q))
    launch(ORDER[2])
    for q in line_peers:
        receive(line.at[q], xs, q, x_peer(q))
    probe_out[pl.ds(my_p * share, share)] = (line[0] + line[1]) + (line[2] + line[3])
    for q in plane_peers:
        send(piece(probe_out, my_p), piece(probe_out, my_p), gs, q, my_p, plane_peer(q))
    launch(ORDER[3])
    for q in plane_peers:
        receive(piece(probe_out, q), gs, q, plane_peer(q))
    for copy in sent:
        copy.wait_send()
    for copy in copies:
        copy.wait()


def send_back(row, side, corner, keep, got):
    chunks = keep.size // (8 * LANE)
    planes = lax.axis_size("col") // 2
    share = chunks // planes
    vmem = pl.BlockSpec(memory_space=pltpu.VMEM)
    dma = lambda n: [pltpu.SemaphoreType.DMA((n,)), pltpu.SemaphoreType.DMA((n,))]
    return pl.pallas_call(
        return_kernel_flat,
        out_shape=tuple(jax.ShapeDtypeStruct(a.shape, a.dtype) for a in (row, side, corner)) + (jax.ShapeDtypeStruct((chunks, 8, LANE), F32),),
        in_specs=[ANY, ANY, ANY, vmem, vmem],
        out_specs=(ANY, ANY, ANY, vmem),
        scratch_shapes=[
            pltpu.VMEM((chunks, 8, LANE), F32),
            pltpu.VMEM((4, share, 8, LANE), F32),
            pltpu.VMEM((planes, share, 8, LANE), F32),
        ]
        + dma(12) + dma(4) + dma(planes) + dma(planes),
        compiler_params=pltpu.CompilerParams(collective_id=3, has_side_effects=True),
        name=NAME,
    )(row, side, corner, keep, got)


def return_kernel_flat(*refs):
    sems = refs[12:]
    return_kernel(*refs[:12], *[sems[i : i + 2] for i in range(0, 8, 2)])


def fold_kernel(halo, centre_ref, row_ref, side_ref, corner_ref, chunks_ref, out_ref, probe_ref, sides, middle, load, store):
    _, r, _ = axis_ids()
    _, _, rows, cols = out_ref.shape
    edge = pl.ds(pl.multiple_of((rows - halo) * (1 - r), halo), halo)
    inner = pl.ds(halo, cols - 2 * halo)
    places = []
    for p in range(2):
        places.append((out_ref.at[p, 0, edge, inner], middle.at[p]))
        for i in range(2):
            places.append((out_ref.at[p, 0, :, pl.ds(i * (cols - halo), halo)], sides.at[i, p]))
    loads = [pltpu.make_async_copy(a, b, load.at[j]) for j, (a, b) in enumerate(places)]
    stores = [pltpu.make_async_copy(b, a, store.at[j]) for j, (a, b) in enumerate(places)]
    for copy in loads:
        copy.start()
    at = 0
    _, half_rows, n = probe_ref.shape
    for p in range(2):
        for t in range(half_rows // 8):
            for h in range(n // LANE):
                probe_ref[p, pl.ds(8 * t, 8), pl.ds(LANE * h, LANE)] = chunks_ref[at]
                at += 1
    for p in range(2):
        loads[3 * p].wait()
        middle[p] += row_ref[p, :, inner].astype(F32)
        stores[3 * p].start()
        for i in range(2):
            loads[3 * p + 1 + i].wait()
            sides[i, p] += side_ref[i, p].astype(F32)
            sides[i, p, edge, :] += row_ref[p, :, pl.ds(i * (cols - halo), halo)].astype(F32) + corner_ref[i, p].astype(F32)
            stores[3 * p + 1 + i].start()
    for copy in stores:
        copy.wait()


def fold(centre, row, side, corner, chunks, n):
    halo = row.shape[1]
    _, _, rows, cols = centre.shape
    vmem = pl.BlockSpec(memory_space=pltpu.VMEM)
    return pl.pallas_call(
        functools.partial(fold_kernel, halo),
        out_shape=(jax.ShapeDtypeStruct(centre.shape, F32), jax.ShapeDtypeStruct((2, n // 2, n), F32)),
        in_specs=[ANY, vmem, vmem, vmem, vmem],
        out_specs=(ANY, vmem),
        scratch_shapes=[
            pltpu.VMEM((2, 2, rows, halo), F32),
            pltpu.VMEM((2, halo, cols - 2 * halo), F32),
            pltpu.SemaphoreType.DMA((6,)),
            pltpu.SemaphoreType.DMA((6,)),
        ],
        input_output_aliases={0: 0},
        name="fold",
    )(centre, row, side, corner, chunks)


def shards(probe, object_re, object_im, phases, centres, occupied, measured):
    n = probe.shape[1]
    _, rows, cols = object_re.shape
    mats, perm = (jnp.asarray(x) for x in constants(n))
    padded, kern, frames = exchange_halo(object_re, object_im, phases, perm, measured, n // 2)
    mine, theirs = extract(centres, occupied, padded, n)
    terms, keep, given = waves(probe, kern, mats, mine, theirs, frames)
    centre, row, side, corner = scatter(centres, terms, rows, cols, n // 2)
    row, side, corner, chunks = send_back(row, side, corner, keep, given)
    return fold(centre, row, side, corner, chunks, n)


def solution(mesh):
    in_specs = (
        P(),
        P("depth", "row", "col"),
        P("depth", "row", "col"),
        P(),
        P("row", "col", None, None, None),
        P("row", "col", None),
        P("row", "col", None, None, None, None),
    )
    out_specs = (P(None, "depth", "row", "col"), P(None, "depth", None))
    return jax.shard_map(shards, mesh=mesh, in_specs=in_specs, out_specs=out_specs, check_vma=False)
```

```python
import functools

import jax
import jax.numpy as jnp
import numpy as np
from jax import lax
from jax.experimental import pallas as pl
from jax.experimental.pallas import tpu as pltpu
from jax.sharding import PartitionSpec as P

MESH = pl.DeviceIdType.MESH
F32 = jnp.float32
BF16 = jnp.bfloat16
ANY = pl.BlockSpec(memory_space=pl.ANY)
LANE = 128
ORDER = ((), (0, 1), (2,), (3,))
REDUCE = True
NAME = 'halo_out'


def constants(n):
    half = n // 2
    k = np.arange(half)
    parts = []
    for parity in range(2):
        turns = (np.outer(2 * k + parity, k) % n) / n
        w = np.exp(-2j * np.pi * turns) / np.sqrt(n)
        block = np.block([[w.real, -w.imag], [w.imag, w.real]])
        for matrix in (block, block.T):
            high = matrix.astype(np.float32).astype(BF16)
            low = (matrix - high.astype(np.float64)).astype(np.float32).astype(BF16)
            parts += [high, low]
    order = np.concatenate([np.arange(0, n, 2), np.arange(1, n, 2)])
    perm = np.zeros((n, n), np.float32)
    perm[np.arange(n), order] = 1.0
    return np.stack(parts), np.stack([perm, perm.T]).astype(BF16)


def axis_ids():
    return lax.axis_index("depth"), lax.axis_index("row"), lax.axis_index("col")


def meet(peers):
    barrier = pltpu.get_barrier_semaphore()
    for peer in peers:
        pl.semaphore_signal(barrier, inc=1, device_id=peer, device_id_type=MESH)
    pl.semaphore_wait(barrier, len(peers))


def remote(src, dst, sems, slot, peer):
    return pltpu.make_async_remote_copy(
        src_ref=src, dst_ref=dst, send_sem=sems[0].at[slot], recv_sem=sems[1].at[slot], device_id=peer, device_id_type=MESH
    )


def neighbours():
    d, r, c = axis_ids()
    cols = lax.axis_size("col")
    right, left = lax.rem(c + 1, cols), lax.rem(c + cols - 1, cols)
    return [(d, 1 - r, c), (d, r, right), (d, r, left), (d, 1 - r, right), (d, 1 - r, left)]


def shifted_in(x, down, right):
    rows, cols = x.shape
    turned = pltpu.roll(x.reshape(rows // 8, 8, cols), jnp.bitwise_and(8 - down, 7), 1)
    sub = lax.broadcasted_iota(jnp.int32, (rows // 8 - 1, 8, cols), 1)
    x = jnp.where(sub < 8 - down, turned[:-1], turned[1:]).reshape(rows - 8, cols)
    turned = [pltpu.roll(x[:, i : i + LANE], jnp.bitwise_and(LANE - right, LANE - 1), 1) for i in range(0, cols, LANE)]
    lanes = lax.broadcasted_iota(jnp.int32, turned[0].shape, 1)
    return jnp.concatenate([jnp.where(lanes < LANE - right, a, b) for a, b in zip(turned[:-1], turned[1:])], 1)


def shifted_out(x, down, right):
    rows, cols = x.shape
    turned = [pltpu.roll(x[:, i : i + LANE], right, 1) for i in range(0, cols, LANE)]
    lanes = lax.broadcasted_iota(jnp.int32, turned[0].shape, 1)
    none = jnp.zeros_like(turned[0])
    x = jnp.concatenate([jnp.where(lanes < right, a, b) for a, b in zip([none] + turned, turned + [none])], 1)
    cols = cols + LANE
    turned = pltpu.roll(x.reshape(rows // 8, 8, cols), down, 1)
    none = jnp.zeros((1, 8, cols), x.dtype)
    sub = lax.broadcasted_iota(jnp.int32, (rows // 8 + 1, 8, cols), 1)
    both = jnp.where(sub < down, jnp.concatenate([none, turned], 0), jnp.concatenate([turned, none], 0))
    return both.reshape(rows + 8, cols)


def split(x):
    high = x.astype(BF16)
    return high, (x - high.astype(F32)).astype(BF16)


def product(a, b, passes):
    (ah, al), (bh, bl) = a, b
    if passes == 3:
        lhs, rhs = [ah, ah, al], [bh, bl, bh]
    else:
        lhs, rhs = [ah], [bh]
    lhs = jnp.concatenate(lhs, 1) if len(lhs) > 1 else lhs[0]
    rhs = jnp.concatenate(rhs, 0) if len(rhs) > 1 else rhs[0]
    return jnp.dot(lhs, rhs, preferred_element_type=F32)


def make_transforms(mats_ref):
    def mat(parity, transposed):
        at = parity * 4 + transposed * 2
        return mats_ref[at], mats_ref[at + 1]

    def left(z, parity, transposed):
        return product(mat(parity, transposed), split(jnp.concatenate(z, 0)), 3)

    def right(z, parity, transposed):
        return product(split(jnp.concatenate(z, 1)), mat(parity, transposed), 3)

    def halves(z):
        h = z.shape[0] // 2
        return z[:h], z[h:]

    def sides(z):
        h = z.shape[1] // 2
        return z[:, :h], z[:, h:]

    def fold(parts, parity):
        return parts[0] + parts[1] if parity == 0 else parts[0] - parts[1]

    def forward(fields):
        outs = [[left([fold(halves(x), parity) for x in z], parity, 0) for parity in range(2)] for z in fields]
        fields = [[jnp.concatenate([halves(o)[i] for o in out], 0) for i in range(2)] for out in outs]
        outs = [[right([fold(sides(x), parity) for x in z], parity, 1) for parity in range(2)] for z in fields]
        return [[jnp.concatenate([sides(o)[i] for o in out], 1) for i in range(2)] for out in outs]

    def inverse(fields):
        outs = [[left([halves(x)[parity] for x in z], parity, 1) for parity in range(2)] for z in fields]
        fields = [[jnp.concatenate([fold([halves(o)[i] for o in out], q) for q in range(2)], 0) for i in range(2)] for out in outs]
        outs = [[right([sides(x)[parity] for x in z], parity, 0) for parity in range(2)] for z in fields]
        return [[jnp.concatenate([fold([sides(o)[i] for o in out], q) for q in range(2)], 1) for i in range(2)] for out in outs]

    return forward, inverse


def cmul(ar, ai, br, bi):
    return ar * br - ai * bi, ar * bi + ai * br


def conj_mul(ar, ai, br, bi):
    return ar * br + ai * bi, ar * bi - ai * br


def rounded(x):
    return x.astype(BF16).astype(F32)


def halo_kernel(half, halo, phases_ref, perm_ref, re_ref, im_ref, frames_ref, pad_ref, kern_ref, ready_ref, stage, frames, phases, perm, kern, ready, send, recv, own):
    d, r, _ = axis_ids()
    _, rows, cols = re_ref.shape
    slots = frames_ref.shape[3]
    batch = half // slots
    peers = neighbours()
    everything, first, last = pl.ds(0, rows), pl.ds(0, halo), pl.ds(cols - halo, halo)
    middle, before, after = pl.ds(halo, cols), pl.ds(0, halo), pl.ds(halo + cols, halo)
    edge = pl.ds(pl.multiple_of((rows - halo) * (1 - r), halo), halo)
    far = pl.ds(pl.multiple_of(rows * r, halo), halo)
    mine = pl.ds(pl.multiple_of(halo * r, halo), rows)
    meet(peers)
    moves = [
        (edge, pl.ds(0, cols), far, middle),
        (everything, last, mine, before),
        (everything, first, mine, after),
        (edge, last, far, before),
        (edge, first, far, after),
    ]
    copies = []
    for p, src in enumerate((re_ref, im_ref)):
        for i, (sr, sc, dr, dc) in enumerate(moves):
            copies.append(remote(src.at[0, sr, sc], pad_ref.at[p, dr, dc], (send, recv), p * 5 + i, peers[i]))
            copies[-1].start()
    sources = [
        (phases_ref, phases),
        (perm_ref, perm),
        (frames_ref.at[0, 0, pl.ds(d * batch, batch)], frames),
        (re_ref.at[0], stage.at[0]),
        (im_ref.at[0], stage.at[1]),
    ]
    targets = [
        (kern, kern_ref),
        (ready, ready_ref),
        (stage.at[0], pad_ref.at[0, mine, middle]),
        (stage.at[1], pad_ref.at[1, mine, middle]),
    ]
    loads = [pltpu.make_async_copy(a, b, own.at[i]) for i, (a, b) in enumerate(sources)]
    stores = [pltpu.make_async_copy(a, b, own.at[5 + i]) for i, (a, b) in enumerate(targets)]
    for load in loads:
        load.start()
    loads[0].wait()
    loads[1].wait()
    kern[0] = reorder(jnp.cos(phases[...]), perm, True)
    kern[1] = reorder(jnp.sin(phases[...]), perm, True)
    stores[0].start()
    for load, store in zip(loads[3:], stores[2:]):
        load.wait()
        store.start()
    loads[2].wait()

    @pl.loop(0, half)
    def _(k):
        ready[k] = reorder(frames[k // slots, lax.rem(k, slots)], perm, True)

    stores[1].start()
    for store in stores:
        store.wait()
    for copy in copies:
        copy.wait()


def exchange_halo(object_re, object_im, phases, perm, measured, halo):
    _, rows, cols = object_re.shape
    batches, slots, n = measured.shape[2:5]
    half = batches * slots // 2
    dma = pltpu.SemaphoreType.DMA
    return pl.pallas_call(
        functools.partial(halo_kernel, half, halo),
        out_shape=(
            jax.ShapeDtypeStruct((2, rows + halo, cols + 2 * halo), BF16),
            jax.ShapeDtypeStruct((2, n, n), F32),
            jax.ShapeDtypeStruct((half, n, n), F32),
        ),
        in_specs=[ANY] * 5,
        out_specs=(ANY,) * 3,
        scratch_shapes=[
            pltpu.VMEM((2, rows, cols), BF16),
            pltpu.VMEM((half // slots, slots, n, n), F32),
            pltpu.VMEM(phases.shape, F32),
            pltpu.VMEM(perm.shape, BF16),
            pltpu.VMEM((2, n, n), F32),
            pltpu.VMEM((half, n, n), F32),
            dma((10,)), dma((10,)), dma((9,)),
        ],
        compiler_params=pltpu.CompilerParams(collective_id=0, has_side_effects=True),
        name="halo_in",
    )(phases, perm, object_re, object_im, measured)


def extract_kernel(halo, centres, occupied, pad_ref, mine_ref, theirs_ref, pieces, wide, load, store, done):
    d, r, _ = axis_ids()
    count = pieces.shape[0]
    half = count // 2
    n = done.shape[-1]
    tall = n + 16
    rows_all = pad_ref.shape[1]
    slots = centres.shape[2]

    def place(k):
        at = jnp.where(k < half, (1 - d) * half + k, d * half + k - half)
        batch, slot = at // slots, lax.rem(at, slots)
        row = centres[0, 0, slot, 0, batch] + halo * (r - 1)
        col = centres[0, 0, slot, 1, batch]
        base = pl.multiple_of(jnp.minimum(row // 16 * 16, rows_all - tall), 16)
        lane = pl.multiple_of(col // LANE * LANE, LANE)
        return base, lane, row - base, col - lane, slot < occupied[0, 0, batch]

    def piece_load(k):
        base, lane, _, _, _ = place(k)
        return pltpu.make_async_copy(pad_ref.at[:, pl.ds(base, tall), pl.ds(lane, n + LANE)], pieces.at[k], load.at[k])

    @pl.loop(0, count)
    def _(k):
        piece_load(k).start()

    def cut(k):
        piece_load(k).wait()
        _, _, down, right, live = place(k)
        skip = pl.multiple_of(down // 8 * 8, 8)
        for p in range(2):
            wide[p, pl.ds(0, tall), :] = pieces[k, p].astype(F32)
            window = shifted_in(wide[p, pl.ds(skip, n + 8), :], down - skip, right)
            done[k, p] = jnp.where(live, window, 0.0).astype(BF16)

    for part, out in enumerate((theirs_ref, mine_ref)):
        @pl.loop(0, half)
        def _(k):
            cut(part * half + k)
            pltpu.make_async_copy(done.at[part * half + k], out.at[k], store.at[part * half + k]).start()

    for part, out in enumerate((theirs_ref, mine_ref)):
        for k in range(half):
            pltpu.make_async_copy(done.at[part * half + k], out.at[k], store.at[part * half + k]).wait()


def extract(centres, occupied, padded, n):
    count = occupied.shape[2] * centres.shape[2]
    half = count // 2
    shape = jax.ShapeDtypeStruct((half, 2, n, n), BF16)
    smem = pl.BlockSpec(memory_space=pltpu.SMEM)
    return pl.pallas_call(
        functools.partial(extract_kernel, n // 2),
        out_shape=(shape, shape),
        in_specs=[smem, smem, ANY],
        out_specs=(ANY, ANY),
        scratch_shapes=[
            pltpu.VMEM((count, 2, n + 16, n + LANE), BF16),
            pltpu.VMEM((2, n + 24, n + LANE), F32),
            pltpu.SemaphoreType.DMA((count,)),
            pltpu.SemaphoreType.DMA((count,)),
            pltpu.VMEM((count, 2, n, n), BF16),
        ],
        name="extract",
    )(centres, occupied, padded)


def reorder(x, perm_ref, both):
    high, low = split(x)
    if both:
        high = jnp.dot(perm_ref[0], high, preferred_element_type=F32).astype(BF16)
        low = jnp.dot(perm_ref[0], low, preferred_element_type=F32).astype(BF16)
    return jnp.dot(high, perm_ref[1], preferred_element_type=F32) + jnp.dot(low, perm_ref[1], preferred_element_type=F32)


def wave_kernel(
    half, probe_hbm, kern_hbm, mats_hbm, mine_ref, theirs_ref, frames_ref,
    terms_ref, keep_ref, given_ref,
    windows, frames, probe_ref, kern, mats_ref, fixed, grads, total, give, own_sem, frame_sem, swap_send, swap_recv, term_send, term_recv, term_own, give_send, give_recv,
):
    d, r, c = axis_ids()
    n = probe_ref.shape[1]
    steady = [pltpu.make_async_copy(a, b, fixed.at[i]) for i, (a, b) in enumerate([(mats_hbm, mats_ref), (probe_hbm, probe_ref), (kern_hbm, kern)])]
    for copy in steady:
        copy.start()
    partner = (1 - d, r, c)

    def own_copy(k):
        return pltpu.make_async_copy(mine_ref.at[k], windows.at[d, k], own_sem.at[k])

    def frame_copy(k):
        return pltpu.make_async_copy(frames_ref.at[k], frames.at[k], frame_sem.at[k])

    def window_copy(k):
        return remote(theirs_ref.at[k], windows.at[d, k], (swap_send, swap_recv), k, partner)

    def term_copies(k):
        there = terms_ref.at[d * half + k]
        return (
            remote(grads.at[1 - d, k], there, (term_send, term_recv), k, partner),
            pltpu.make_async_copy(grads.at[d, k], there, term_own.at[k]),
        )

    @pl.loop(0, half)
    def _(k):
        own_copy(k).start()
        frame_copy(k).start()

    meet([partner])

    @pl.loop(0, half)
    def _(k):
        window_copy(k).start()

    total[...] = jnp.zeros_like(total)
    forward, inverse = make_transforms(mats_ref)
    for copy in steady:
        copy.wait()

    group = 2

    @pl.loop(0, half // group)
    def _(step):
        ks = [step * group + i for i in range(group)]

        def window(s, k):
            return [windows[s, k, p].astype(F32) for p in range(2)]

        for k in ks:
            own_copy(k).wait()
            frame_copy(k).wait()
            window_copy(k).wait()
        waves = forward([cmul(probe_ref[0], probe_ref[1], *window(0, k)) for k in ks])
        waves = inverse([cmul(fr, fi, kern[0], kern[1]) for fr, fi in waves])
        waves = [(rounded(pr), rounded(pi)) for pr, pi in waves]
        fields = forward([cmul(*wave, *window(1, k)) for wave, k in zip(waves, ks)])
        misfits = [fr * fr + fi * fi - frames[k] for (fr, fi), k in zip(fields, ks)]
        fields = inverse([(m * fr, m * fi) for (fr, fi), m in zip(fields, misfits)])
        for k, wave, field in zip(ks, waves, fields):
            gr, gi = conj_mul(*wave, *field)
            grads[1, k, 0] = gr.astype(BF16)
            grads[1, k, 1] = gi.astype(BF16)
        fields = forward([conj_mul(*window(1, k), *field) for k, field in zip(ks, fields)])
        fields = inverse([conj_mul(kern[0], kern[1], *field) for field in fields])
        fields = [(rounded(xr), rounded(xi)) for xr, xi in fields]
        for k, field in zip(ks, fields):
            gr, gi = conj_mul(probe_ref[0], probe_ref[1], *field)
            grads[0, k, 0] = gr.astype(BF16)
            grads[0, k, 1] = gi.astype(BF16)
            lr, li = conj_mul(*window(0, k), *field)
            total[0] += lr
            total[1] += li
        for k in ks:
            for copy in term_copies(k):
                copy.start()

    mid = n // 2
    for p in range(2):
        give[p] = total[p, pl.ds(pl.multiple_of((1 - d) * mid, 8), mid), :].astype(BF16)
        keep_ref[p] = total[p, pl.ds(pl.multiple_of(d * mid, 8), mid), :]
    last_copy = pltpu.make_async_remote_copy(give, given_ref, give_send, give_recv, device_id=partner, device_id_type=MESH)
    last_copy.start()

    @pl.loop(0, half)
    def _(k):
        for copy in term_copies(k):
            copy.wait()

    last_copy.wait()


def waves(probe, kern, mats, mine, theirs, frames):
    half, _, n, _ = mine.shape
    vmem = pl.BlockSpec(memory_space=pltpu.VMEM)
    dma = pltpu.SemaphoreType.DMA
    return pl.pallas_call(
        functools.partial(wave_kernel, half),
        out_shape=(
            jax.ShapeDtypeStruct((2 * half, 2, n, n), BF16),
            jax.ShapeDtypeStruct((2, n // 2, n), F32),
            jax.ShapeDtypeStruct((2, n // 2, n), BF16),
        ),
        in_specs=[ANY] * 6,
        out_specs=(ANY, vmem, ANY),
        scratch_shapes=[
            pltpu.VMEM((2, half, 2, n, n), BF16),
            pltpu.VMEM((half, n, n), F32),
            pltpu.VMEM(probe.shape, F32),
            pltpu.VMEM(kern.shape, F32),
            pltpu.VMEM(mats.shape, BF16),
            dma((3,)),
            pltpu.VMEM((2, half, 2, n, n), BF16),
            pltpu.VMEM((2, n, n), F32),
            pltpu.VMEM((2, n // 2, n), BF16),
        ]
        + [dma((half,))] * 7 + [dma(()), dma(())],
        compiler_params=pltpu.CompilerParams(collective_id=1, has_side_effects=True),
        name="waves",
    )(probe, kern, mats, mine, theirs, frames)


def scatter_kernel(halo, centres, terms_ref, centre_ref, row_ref, side_ref, corner_ref, terms, acc, row_buf, side_buf, corner_buf, load, store):
    _, r, _ = axis_ids()
    count, _, n, _ = terms.shape
    _, _, rows, cols = centre_ref.shape
    slots = centres.shape[2]

    def term_load(p, k):
        return pltpu.make_async_copy(terms_ref.at[k, p], terms.at[k, p], load.at[p, k])

    for p in range(2):
        for k in range(count):
            term_load(p, k).start()
    mine = pl.ds(pl.multiple_of(halo * r, halo), rows)
    far = pl.ds(pl.multiple_of(rows * (1 - r), halo), halo)
    stores = []

    def put(src, dst):
        stores.append(pltpu.make_async_copy(src, dst, store.at[len(stores)]))
        stores[-1].start()

    for p in range(2):
        acc[p] = jnp.zeros(acc.shape[1:], F32)

        @pl.loop(0, count)
        def _(k):
            term_load(p, k).wait()
            row = centres[0, 0, lax.rem(k, slots), 0, k // slots] + halo * (r - 1)
            col = centres[0, 0, lax.rem(k, slots), 1, k // slots]
            top = pl.multiple_of(row // 8 * 8, 8)
            lane = pl.multiple_of(col // LANE * LANE, LANE)
            acc[p, pl.ds(top, n + 8), pl.ds(lane, n + LANE)] += shifted_out(terms[k, p].astype(F32), row - top, col - lane)

        put(acc.at[p, mine, pl.ds(halo, cols)], centre_ref.at[p, 0])
        row_buf[p] = acc[p, far, pl.ds(halo, cols)].astype(BF16)
        put(row_buf.at[p], row_ref.at[p])
        for i, at in enumerate((halo + cols, 0)):
            side_buf[i, p] = acc[p, mine, pl.ds(at, halo)].astype(BF16)
            put(side_buf.at[i, p], side_ref.at[i, p])
            corner_buf[i, p] = acc[p, far, pl.ds(at, halo)].astype(BF16)
            put(corner_buf.at[i, p], corner_ref.at[i, p])
    for copy in stores:
        copy.wait()


def scatter(centres, terms, rows, cols, halo):
    count, _, n, _ = terms.shape
    shapes = [((2, 1, rows, cols), F32), ((2, halo, cols), BF16), ((2, 2, rows, halo), BF16), ((2, 2, halo, halo), BF16)]
    return pl.pallas_call(
        functools.partial(scatter_kernel, halo),
        out_shape=tuple(jax.ShapeDtypeStruct(s, t) for s, t in shapes),
        in_specs=[pl.BlockSpec(memory_space=pltpu.SMEM), ANY],
        out_specs=(ANY,) * 4,
        scratch_shapes=[
            pltpu.VMEM(terms.shape, BF16),
            pltpu.VMEM((2, rows + halo + 8, cols + 2 * halo), F32),
        ]
        + [pltpu.VMEM(s, t) for s, t in shapes[1:]]
        + [pltpu.SemaphoreType.DMA((2, count)), pltpu.SemaphoreType.DMA((12,))],
        name="scatter",
    )(centres, terms)


def x_peer(q):
    d, _, c = axis_ids()
    return (d, q // 2, c // 2 * 2 + lax.rem(q, 2))


def plane_peer(q):
    d, r, c = axis_ids()
    return (d, r, q * 2 + lax.rem(c, 2))


def return_kernel(row_ref, side_ref, corner_ref, keep_hbm, got_hbm, row_out, side_out, corner_out, probe_out, keep_ref, got_ref, buf, line, plane, final, local, strips, xs, ps, gs):
    d, r, c = axis_ids()
    planes = lax.axis_size("col") // 2
    my_x = r * 2 + lax.rem(c, 2)
    my_p = c // 2
    peers = neighbours()
    line_peers = [lax.rem(my_x + t, 4) for t in range(1, 4)]
    plane_peers = [lax.rem(my_p + t, planes) for t in range(1, planes)]
    loads = [pltpu.make_async_copy(a, b, local.at[i]) for i, (a, b) in enumerate([(keep_hbm, keep_ref), (got_hbm, got_ref)])]
    for load in loads:
        load.start()
    meet(peers + [x_peer(q) for q in line_peers] + [plane_peer(q) for q in plane_peers])
    wide = row_ref.shape[-1] // 2
    groups = [[] for _ in range(4)]
    for p in range(2):
        for i in range(2):
            part = (p, slice(None), pl.ds(i * wide, wide))
            groups[2 * p + i].append((row_ref.at[part], row_out.at[part], peers[0]))
            groups[2 * p + i].append((side_ref.at[i, p], side_out.at[i, p], peers[1 + i]))
            groups[2 * p + i].append((corner_ref.at[i, p], corner_out.at[i, p], peers[3 + i]))
    copies = []

    def launch(chosen):
        for s, t, peer in [m for g in chosen for m in groups[g]]:
            copies.append(remote(s, t, strips, len(copies), peer))
            copies[-1].start()

    for load in loads:
        load.wait()
    half_rows, n = keep_ref.shape[1:]
    at = 0
    for p in range(2):
        for t in range(half_rows // 8):
            for h in range(n // LANE):
                place = (p, pl.ds(8 * t, 8), pl.ds(LANE * h, LANE))
                buf[at] = keep_ref[place] + got_ref[place].astype(F32)
                at += 1
    share = at // planes

    def piece(ref, q):
        return ref.at[pl.ds(q * share, share)]

    def send(src, dst, sems, q, me, peer):
        copy = pltpu.make_async_remote_copy(src, dst, sems[0].at[q], sems[1].at[me], device_id=peer, device_id_type=MESH)
        copy.start()
        sent.append(copy)

    def receive(dst, sems, q, peer):
        pltpu.make_async_remote_copy(dst, dst, sems[0].at[q], sems[1].at[q], device_id=peer, device_id_type=MESH).wait_recv()

    sent = []
    launch(ORDER[0])
    for q in plane_peers:
        send(piece(buf, q), plane.at[my_p], ps, q, my_p, plane_peer(q))
    launch(ORDER[1])
    for q in plane_peers:
        receive(plane.at[q], ps, q, plane_peer(q))
    total = buf[pl.ds(my_p * share, share)]
    for q in plane_peers:
        total = total + plane[q]
    line[my_x] = total
    for q in line_peers:
        send(line.at[my_x], line.at[my_x], xs, q, my_x, x_peer(q))
    launch(ORDER[2])
    for q in line_peers:
        receive(line.at[q], xs, q, x_peer(q))
    final[...] = (line[0] + line[1]) + (line[2] + line[3])
    own = pltpu.make_async_copy(final, piece(probe_out, my_p), local.at[2])
    own.start()
    for q in plane_peers:
        send(final, piece(probe_out, my_p), gs, q, my_p, plane_peer(q))
    launch(ORDER[3])
    for q in plane_peers:
        receive(piece(probe_out, q), gs, q, plane_peer(q))
    own.wait()
    for copy in sent:
        copy.wait_send()
    for copy in copies:
        copy.wait()


def send_back(row, side, corner, keep, got):
    chunks = keep.size // (8 * LANE)
    planes = lax.axis_size("col") // 2
    share = chunks // planes
    dma = lambda n: [pltpu.SemaphoreType.DMA((n,)), pltpu.SemaphoreType.DMA((n,))]
    return pl.pallas_call(
        return_kernel_flat,
        out_shape=tuple(jax.ShapeDtypeStruct(a.shape, a.dtype) for a in (row, side, corner)) + (jax.ShapeDtypeStruct((chunks, 8, LANE), F32),),
        in_specs=[ANY] * 5,
        out_specs=(ANY,) * 4,
        scratch_shapes=[
            pltpu.VMEM(keep.shape, F32),
            pltpu.VMEM(got.shape, BF16),
            pltpu.VMEM((chunks, 8, LANE), F32),
            pltpu.VMEM((4, share, 8, LANE), F32),
            pltpu.VMEM((planes, share, 8, LANE), F32),
            pltpu.VMEM((share, 8, LANE), F32),
            pltpu.SemaphoreType.DMA((3,)),
        ]
        + dma(12) + dma(4) + dma(planes) + dma(planes),
        compiler_params=pltpu.CompilerParams(collective_id=3, has_side_effects=True),
        name=NAME,
    )(row, side, corner, keep, got)


def return_kernel_flat(*refs):
    sems = refs[16:]
    return_kernel(*refs[:16], *[sems[i : i + 2] for i in range(0, 8, 2)])


def fold_kernel(halo, centre_ref, row_hbm, side_hbm, corner_hbm, chunks_hbm, out_ref, probe_out, sides, middle, row_ref, side_ref, corner_ref, chunks_ref, probe_ref, load, extra, store):
    _, r, _ = axis_ids()
    _, _, rows, cols = out_ref.shape
    edge = pl.ds(pl.multiple_of((rows - halo) * (1 - r), halo), halo)
    inner = pl.ds(halo, cols - 2 * halo)
    strips = [(row_hbm, row_ref), (side_hbm, side_ref), (corner_hbm, corner_ref), (chunks_hbm, chunks_ref)]
    places = []
    for p in range(2):
        places.append((out_ref.at[p, 0, edge, inner], middle.at[p]))
        for i in range(2):
            places.append((out_ref.at[p, 0, :, pl.ds(i * (cols - halo), halo)], sides.at[i, p]))
    brought = [pltpu.make_async_copy(a, b, extra.at[j]) for j, (a, b) in enumerate(strips)]
    loads = [pltpu.make_async_copy(a, b, load.at[j]) for j, (a, b) in enumerate(places)]
    stores = [pltpu.make_async_copy(b, a, store.at[j]) for j, (a, b) in enumerate(places)]
    stores.append(pltpu.make_async_copy(probe_ref, probe_out, store.at[len(places)]))
    brought[0].start()
    loads[0].start()
    brought[1].start()
    brought[2].start()
    for copy in loads[1:]:
        copy.start()
    brought[3].start()
    for copy in brought[:3]:
        copy.wait()
    for p in range(2):
        loads[3 * p].wait()
        middle[p] += row_ref[p, :, inner].astype(F32)
        stores[3 * p].start()
        for i in range(2):
            loads[3 * p + 1 + i].wait()
            sides[i, p] += side_ref[i, p].astype(F32)
            sides[i, p, edge, :] += row_ref[p, :, pl.ds(i * (cols - halo), halo)].astype(F32) + corner_ref[i, p].astype(F32)
            stores[3 * p + 1 + i].start()
    brought[3].wait()
    at = 0
    _, half_rows, n = probe_ref.shape
    for p in range(2):
        for t in range(half_rows // 8):
            for h in range(n // LANE):
                probe_ref[p, pl.ds(8 * t, 8), pl.ds(LANE * h, LANE)] = chunks_ref[at]
                at += 1
    stores[-1].start()
    for copy in stores:
        copy.wait()


def fold(centre, row, side, corner, chunks, n):
    halo = row.shape[1]
    _, _, rows, cols = centre.shape
    return pl.pallas_call(
        functools.partial(fold_kernel, halo),
        out_shape=(jax.ShapeDtypeStruct(centre.shape, F32), jax.ShapeDtypeStruct((2, n // 2, n), F32)),
        in_specs=[ANY] * 5,
        out_specs=(ANY, ANY),
        scratch_shapes=[
            pltpu.VMEM((2, 2, rows, halo), F32),
            pltpu.VMEM((2, halo, cols - 2 * halo), F32),
        ]
        + [pltpu.VMEM(a.shape, a.dtype) for a in (row, side, corner, chunks)]
        + [pltpu.VMEM((2, n // 2, n), F32)]
        + [pltpu.SemaphoreType.DMA((6,)), pltpu.SemaphoreType.DMA((4,)), pltpu.SemaphoreType.DMA((7,))],
        input_output_aliases={0: 0},
        name="fold",
    )(centre, row, side, corner, chunks)


def shards(probe, object_re, object_im, phases, centres, occupied, measured):
    n = probe.shape[1]
    _, rows, cols = object_re.shape
    mats, perm = (jnp.asarray(x) for x in constants(n))
    centres = jnp.transpose(centres, (0, 1, 3, 4, 2))
    padded, kern, frames = exchange_halo(object_re, object_im, phases, perm, measured, n // 2)
    mine, theirs = extract(centres, occupied, padded, n)
    terms, keep, given = waves(probe, kern, mats, mine, theirs, frames)
    centre, row, side, corner = scatter(centres, terms, rows, cols, n // 2)
    row, side, corner, chunks = send_back(row, side, corner, keep, given)
    return fold(centre, row, side, corner, chunks, n)


def solution(mesh):
    in_specs = (
        P(),
        P("depth", "row", "col"),
        P("depth", "row", "col"),
        P(),
        P("row", "col", None, None, None),
        P("row", "col", None),
        P("row", "col", None, None, None, None),
    )
    out_specs = (P(None, "depth", "row", "col"), P(None, "depth", None))
    return jax.shard_map(shards, mesh=mesh, in_specs=in_specs, out_specs=out_specs, check_vma=False)
```

```python
import functools

import jax
import jax.numpy as jnp
import numpy as np
from jax import lax
from jax.experimental import pallas as pl
from jax.experimental.pallas import tpu as pltpu
from jax.sharding import PartitionSpec as P

MESH = pl.DeviceIdType.MESH
F32 = jnp.float32
BF16 = jnp.bfloat16
ANY = pl.BlockSpec(memory_space=pl.ANY)
LANE = 128
ORDER = ((0,), (1,), (2,), (3,))
REDUCE = True
NAME = 'halo_out'


def constants(n):
    half = n // 2
    k = np.arange(half)
    parts = []
    for parity in range(2):
        turns = (np.outer(2 * k + parity, k) % n) / n
        w = np.exp(-2j * np.pi * turns) / np.sqrt(n)
        block = np.block([[w.real, -w.imag], [w.imag, w.real]])
        for matrix in (block, block.T):
            high = matrix.astype(np.float32).astype(BF16)
            low = (matrix - high.astype(np.float64)).astype(np.float32).astype(BF16)
            parts += [high, low]
    order = np.concatenate([np.arange(0, n, 2), np.arange(1, n, 2)])
    perm = np.zeros((n, n), np.float32)
    perm[np.arange(n), order] = 1.0
    return np.stack(parts), np.stack([perm, perm.T]).astype(BF16)


def axis_ids():
    return lax.axis_index("depth"), lax.axis_index("row"), lax.axis_index("col")


def meet(peers):
    barrier = pltpu.get_barrier_semaphore()
    for peer in peers:
        pl.semaphore_signal(barrier, inc=1, device_id=peer, device_id_type=MESH)
    pl.semaphore_wait(barrier, len(peers))


def remote(src, dst, sems, slot, peer):
    return pltpu.make_async_remote_copy(
        src_ref=src, dst_ref=dst, send_sem=sems[0].at[slot], recv_sem=sems[1].at[slot], device_id=peer, device_id_type=MESH
    )


def neighbours():
    d, r, c = axis_ids()
    cols = lax.axis_size("col")
    right, left = lax.rem(c + 1, cols), lax.rem(c + cols - 1, cols)
    return [(d, 1 - r, c), (d, r, right), (d, r, left), (d, 1 - r, right), (d, 1 - r, left)]


def shifted_in(x, down, right):
    rows, cols = x.shape
    turned = pltpu.roll(x.reshape(rows // 8, 8, cols), jnp.bitwise_and(8 - down, 7), 1)
    sub = lax.broadcasted_iota(jnp.int32, (rows // 8 - 1, 8, cols), 1)
    x = jnp.where(sub < 8 - down, turned[:-1], turned[1:]).reshape(rows - 8, cols)
    turned = [pltpu.roll(x[:, i : i + LANE], jnp.bitwise_and(LANE - right, LANE - 1), 1) for i in range(0, cols, LANE)]
    lanes = lax.broadcasted_iota(jnp.int32, turned[0].shape, 1)
    return jnp.concatenate([jnp.where(lanes < LANE - right, a, b) for a, b in zip(turned[:-1], turned[1:])], 1)


def shifted_out(x, down, right):
    rows, cols = x.shape
    turned = [pltpu.roll(x[:, i : i + LANE], right, 1) for i in range(0, cols, LANE)]
    lanes = lax.broadcasted_iota(jnp.int32, turned[0].shape, 1)
    none = jnp.zeros_like(turned[0])
    x = jnp.concatenate([jnp.where(lanes < right, a, b) for a, b in zip([none] + turned, turned + [none])], 1)
    cols = cols + LANE
    turned = pltpu.roll(x.reshape(rows // 8, 8, cols), down, 1)
    none = jnp.zeros((1, 8, cols), x.dtype)
    sub = lax.broadcasted_iota(jnp.int32, (rows // 8 + 1, 8, cols), 1)
    both = jnp.where(sub < down, jnp.concatenate([none, turned], 0), jnp.concatenate([turned, none], 0))
    return both.reshape(rows + 8, cols)


def split(x):
    high = x.astype(BF16)
    return high, (x - high.astype(F32)).astype(BF16)


def make_transforms(mats_ref):
    def mat(parity, transposed):
        at = parity * 4 + transposed * 2
        return mats_ref[at], mats_ref[at + 1]

    def left(z, parity, transposed, exact):
        high, low = mat(parity, transposed)
        zh, zl = split(jnp.concatenate(z, 0))
        if not exact:
            return jnp.dot(jnp.concatenate([high, high], 1), jnp.concatenate([zh, zl], 0), preferred_element_type=F32)
        out = jnp.dot(jnp.concatenate([high, low], 0), zh, preferred_element_type=F32)
        n = out.shape[0] // 2
        return out[:n] + (out[n:] + jnp.dot(high, zl, preferred_element_type=F32))

    def right(z, parity, transposed, exact):
        high, low = mat(parity, transposed)
        zh, zl = split(jnp.concatenate(z, 1))
        if not exact:
            out = jnp.dot(jnp.concatenate([zh, zl], 0), high, preferred_element_type=F32)
            n = out.shape[0] // 2
            return out[:n] + out[n:]
        out = jnp.dot(jnp.concatenate([zh, zl], 0), high, preferred_element_type=F32)
        n = out.shape[0] // 2
        return out[:n] + (out[n:] + jnp.dot(zh, low, preferred_element_type=F32))

    def halves(z):
        h = z.shape[0] // 2
        return z[:h], z[h:]

    def sides(z):
        h = z.shape[1] // 2
        return z[:, :h], z[:, h:]

    def fold(parts, parity):
        return parts[0] + parts[1] if parity == 0 else parts[0] - parts[1]

    def forward(fields, exact=True):
        outs = [[left([fold(halves(x), parity) for x in z], parity, 0, exact) for parity in range(2)] for z in fields]
        fields = [[jnp.concatenate([halves(o)[i] for o in out], 0) for i in range(2)] for out in outs]
        outs = [[right([fold(sides(x), parity) for x in z], parity, 1, exact) for parity in range(2)] for z in fields]
        return [[jnp.concatenate([sides(o)[i] for o in out], 1) for i in range(2)] for out in outs]

    def inverse(fields, exact=True):
        outs = [[left([halves(x)[parity] for x in z], parity, 1, exact) for parity in range(2)] for z in fields]
        fields = [[jnp.concatenate([fold([halves(o)[i] for o in out], q) for q in range(2)], 0) for i in range(2)] for out in outs]
        outs = [[right([sides(x)[parity] for x in z], parity, 0, exact) for parity in range(2)] for z in fields]
        return [[jnp.concatenate([fold([sides(o)[i] for o in out], q) for q in range(2)], 1) for i in range(2)] for out in outs]

    return forward, inverse


def cmul(ar, ai, br, bi):
    return ar * br - ai * bi, ar * bi + ai * br


def conj_mul(ar, ai, br, bi):
    return ar * br + ai * bi, ar * bi - ai * br


def rounded(x):
    return x.astype(BF16).astype(F32)


def halo_kernel(half, halo, phases_ref, perm_ref, re_ref, im_ref, frames_ref, pad_ref, kern_ref, ready_ref, stage, frames, phases, perm, kern, ready, send, recv, own):
    d, r, _ = axis_ids()
    _, rows, cols = re_ref.shape
    slots = frames_ref.shape[3]
    batch = half // slots
    peers = neighbours()
    everything, first, last = pl.ds(0, rows), pl.ds(0, halo), pl.ds(cols - halo, halo)
    middle, before, after = pl.ds(halo, cols), pl.ds(0, halo), pl.ds(halo + cols, halo)
    edge = pl.ds(pl.multiple_of((rows - halo) * (1 - r), halo), halo)
    far = pl.ds(pl.multiple_of(rows * r, halo), halo)
    mine = pl.ds(pl.multiple_of(halo * r, halo), rows)
    meet(peers)
    moves = [
        (edge, pl.ds(0, cols), far, middle),
        (everything, last, mine, before),
        (everything, first, mine, after),
        (edge, last, far, before),
        (edge, first, far, after),
    ]
    copies = []
    for p, src in enumerate((re_ref, im_ref)):
        for i, (sr, sc, dr, dc) in enumerate(moves):
            copies.append(remote(src.at[0, sr, sc], pad_ref.at[p, dr, dc], (send, recv), p * 5 + i, peers[i]))
            copies[-1].start()
    sources = [
        (phases_ref, phases),
        (perm_ref, perm),
        (frames_ref.at[0, 0, pl.ds(d * batch, batch)], frames),
        (re_ref.at[0], stage.at[0]),
        (im_ref.at[0], stage.at[1]),
    ]
    targets = [
        (kern, kern_ref),
        (ready, ready_ref),
        (stage.at[0], pad_ref.at[0, mine, middle]),
        (stage.at[1], pad_ref.at[1, mine, middle]),
    ]
    loads = [pltpu.make_async_copy(a, b, own.at[i]) for i, (a, b) in enumerate(sources)]
    stores = [pltpu.make_async_copy(a, b, own.at[5 + i]) for i, (a, b) in enumerate(targets)]
    for load in loads:
        load.start()
    loads[0].wait()
    loads[1].wait()
    kern[0] = reorder(jnp.cos(phases[...]), perm, True)
    kern[1] = reorder(jnp.sin(phases[...]), perm, True)
    stores[0].start()
    for load, store in zip(loads[3:], stores[2:]):
        load.wait()
        store.start()
    loads[2].wait()

    @pl.loop(0, half)
    def _(k):
        ready[k] = reorder(frames[k // slots, lax.rem(k, slots)], perm, True)

    stores[1].start()
    for store in stores:
        store.wait()
    for copy in copies:
        copy.wait()


def exchange_halo(object_re, object_im, phases, perm, measured, halo):
    _, rows, cols = object_re.shape
    batches, slots, n = measured.shape[2:5]
    half = batches * slots // 2
    dma = pltpu.SemaphoreType.DMA
    return pl.pallas_call(
        functools.partial(halo_kernel, half, halo),
        out_shape=(
            jax.ShapeDtypeStruct((2, rows + halo, cols + 2 * halo), BF16),
            jax.ShapeDtypeStruct((2, n, n), F32),
            jax.ShapeDtypeStruct((half, n, n), F32),
        ),
        in_specs=[ANY] * 5,
        out_specs=(ANY,) * 3,
        scratch_shapes=[
            pltpu.VMEM((2, rows, cols), BF16),
            pltpu.VMEM((half // slots, slots, n, n), F32),
            pltpu.VMEM(phases.shape, F32),
            pltpu.VMEM(perm.shape, BF16),
            pltpu.VMEM((2, n, n), F32),
            pltpu.VMEM((half, n, n), F32),
            dma((10,)), dma((10,)), dma((9,)),
        ],
        compiler_params=pltpu.CompilerParams(collective_id=0, has_side_effects=True),
        name="halo_in",
    )(phases, perm, object_re, object_im, measured)


def extract_kernel(halo, centres, occupied, pad_ref, mine_ref, theirs_ref, pieces, wide, load, store, done):
    d, r, _ = axis_ids()
    count = pieces.shape[0]
    half = count // 2
    n = done.shape[-1]
    tall = n + 16
    rows_all = pad_ref.shape[1]
    slots = centres.shape[2]

    def place(k):
        at = jnp.where(k < half, (1 - d) * half + k, d * half + k - half)
        batch, slot = at // slots, lax.rem(at, slots)
        row = centres[0, 0, slot, 0, batch] + halo * (r - 1)
        col = centres[0, 0, slot, 1, batch]
        base = pl.multiple_of(jnp.minimum(row // 16 * 16, rows_all - tall), 16)
        lane = pl.multiple_of(col // LANE * LANE, LANE)
        return base, lane, row - base, col - lane, slot < occupied[0, 0, batch]

    def piece_load(k):
        base, lane, _, _, _ = place(k)
        return pltpu.make_async_copy(pad_ref.at[:, pl.ds(base, tall), pl.ds(lane, n + LANE)], pieces.at[k], load.at[k])

    @pl.loop(0, count)
    def _(k):
        piece_load(k).start()

    def cut(k):
        piece_load(k).wait()
        _, _, down, right, live = place(k)
        skip = pl.multiple_of(down // 8 * 8, 8)
        for p in range(2):
            wide[p, pl.ds(0, tall), :] = pieces[k, p].astype(F32)
            window = shifted_in(wide[p, pl.ds(skip, n + 8), :], down - skip, right)
            done[k, p] = jnp.where(live, window, 0.0).astype(BF16)

    for part, out in enumerate((theirs_ref, mine_ref)):
        @pl.loop(0, half)
        def _(k):
            cut(part * half + k)
            pltpu.make_async_copy(done.at[part * half + k], out.at[k], store.at[part * half + k]).start()

    for part, out in enumerate((theirs_ref, mine_ref)):
        for k in range(half):
            pltpu.make_async_copy(done.at[part * half + k], out.at[k], store.at[part * half + k]).wait()


def extract(centres, occupied, padded, n):
    count = occupied.shape[2] * centres.shape[2]
    half = count // 2
    shape = jax.ShapeDtypeStruct((half, 2, n, n), BF16)
    smem = pl.BlockSpec(memory_space=pltpu.SMEM)
    return pl.pallas_call(
        functools.partial(extract_kernel, n // 2),
        out_shape=(shape, shape),
        in_specs=[smem, smem, ANY],
        out_specs=(ANY, ANY),
        scratch_shapes=[
            pltpu.VMEM((count, 2, n + 16, n + LANE), BF16),
            pltpu.VMEM((2, n + 24, n + LANE), F32),
            pltpu.SemaphoreType.DMA((count,)),
            pltpu.SemaphoreType.DMA((count,)),
            pltpu.VMEM((count, 2, n, n), BF16),
        ],
        name="extract",
    )(centres, occupied, padded)


def reorder(x, perm_ref, both):
    high, low = split(x)
    if both:
        high = jnp.dot(perm_ref[0], high, preferred_element_type=F32).astype(BF16)
        low = jnp.dot(perm_ref[0], low, preferred_element_type=F32).astype(BF16)
    return jnp.dot(high, perm_ref[1], preferred_element_type=F32) + jnp.dot(low, perm_ref[1], preferred_element_type=F32)


def wave_kernel(
    half, probe_hbm, kern_hbm, mats_hbm, mine_ref, theirs_ref, frames_ref,
    terms_ref, total_ref,
    windows, frames, probe_ref, kern, mats_ref, fixed, grads, total, own_sem, frame_sem, swap_send, swap_recv, term_send, term_recv, term_own, total_sem,
):
    d, r, c = axis_ids()
    n = probe_ref.shape[1]
    steady = [pltpu.make_async_copy(a, b, fixed.at[i]) for i, (a, b) in enumerate([(mats_hbm, mats_ref), (probe_hbm, probe_ref), (kern_hbm, kern)])]
    for copy in steady:
        copy.start()
    partner = (1 - d, r, c)

    def own_copy(k):
        return pltpu.make_async_copy(mine_ref.at[k], windows.at[d, k], own_sem.at[k])

    def frame_copy(k):
        return pltpu.make_async_copy(frames_ref.at[k], frames.at[k], frame_sem.at[k])

    def window_copy(k):
        return remote(theirs_ref.at[k], windows.at[d, k], (swap_send, swap_recv), k, partner)

    def term_copies(k):
        there = terms_ref.at[d * half + k]
        return (
            remote(grads.at[1 - d, k], there, (term_send, term_recv), k, partner),
            pltpu.make_async_copy(grads.at[d, k], there, term_own.at[k]),
        )

    @pl.loop(0, half)
    def _(k):
        own_copy(k).start()

    meet([partner])

    @pl.loop(0, half)
    def _(k):
        window_copy(k).start()
        frame_copy(k).start()

    total[...] = jnp.zeros_like(total)
    forward, inverse = make_transforms(mats_ref)
    for copy in steady:
        copy.wait()

    group = 2

    @pl.loop(0, half // group)
    def _(step):
        ks = [step * group + i for i in range(group)]

        def window(s, k):
            return [windows[s, k, p].astype(F32) for p in range(2)]

        for k in ks:
            own_copy(k).wait()
            frame_copy(k).wait()
            window_copy(k).wait()
        waves = forward([cmul(probe_ref[0], probe_ref[1], *window(0, k)) for k in ks])
        waves = inverse([cmul(fr, fi, kern[0], kern[1]) for fr, fi in waves])
        waves = [(rounded(pr), rounded(pi)) for pr, pi in waves]
        fields = forward([cmul(*wave, *window(1, k)) for wave, k in zip(waves, ks)])
        misfits = [fr * fr + fi * fi - frames[k] for (fr, fi), k in zip(fields, ks)]
        fields = inverse([(m * fr, m * fi) for (fr, fi), m in zip(fields, misfits)], False)
        for k, wave, field in zip(ks, waves, fields):
            gr, gi = conj_mul(*wave, *field)
            grads[1, k, 0] = gr.astype(BF16)
            grads[1, k, 1] = gi.astype(BF16)
        fields = forward([conj_mul(*window(1, k), *field) for k, field in zip(ks, fields)], False)
        fields = inverse([conj_mul(kern[0], kern[1], *field) for field in fields], False)
        fields = [(rounded(xr), rounded(xi)) for xr, xi in fields]
        for k, field in zip(ks, fields):
            gr, gi = conj_mul(probe_ref[0], probe_ref[1], *field)
            grads[0, k, 0] = gr.astype(BF16)
            grads[0, k, 1] = gi.astype(BF16)
            lr, li = conj_mul(*window(0, k), *field)
            total[0] += lr
            total[1] += li
            for copy in term_copies(k):
                copy.start()

    last_copy = pltpu.make_async_copy(total, total_ref, total_sem)
    last_copy.start()

    @pl.loop(0, half)
    def _(k):
        for copy in term_copies(k):
            copy.wait()

    last_copy.wait()


def waves(probe, kern, mats, mine, theirs, frames):
    half, _, n, _ = mine.shape
    dma = pltpu.SemaphoreType.DMA
    return pl.pallas_call(
        functools.partial(wave_kernel, half),
        out_shape=(
            jax.ShapeDtypeStruct((2 * half, 2, n, n), BF16),
            jax.ShapeDtypeStruct((2, n, n), F32),
        ),
        in_specs=[ANY] * 6,
        out_specs=(ANY, ANY),
        scratch_shapes=[
            pltpu.VMEM((2, half, 2, n, n), BF16),
            pltpu.VMEM((half, n, n), F32),
            pltpu.VMEM(probe.shape, F32),
            pltpu.VMEM(kern.shape, F32),
            pltpu.VMEM(mats.shape, BF16),
            dma((3,)),
            pltpu.VMEM((2, half, 2, n, n), BF16),
            pltpu.VMEM((2, n, n), F32),
        ]
        + [dma((half,))] * 7 + [dma(())],
        compiler_params=pltpu.CompilerParams(collective_id=1, has_side_effects=True),
        name="waves",
    )(probe, kern, mats, mine, theirs, frames)


def scatter_kernel(halo, centres, terms_ref, centre_ref, row_ref, side_ref, corner_ref, terms, acc, row_buf, side_buf, corner_buf, load, store):
    _, r, _ = axis_ids()
    count, _, n, _ = terms.shape
    _, _, rows, cols = centre_ref.shape
    slots = centres.shape[2]

    def term_load(p, k):
        return pltpu.make_async_copy(terms_ref.at[k, p], terms.at[k, p], load.at[p, k])

    for p in range(2):
        for k in range(count):
            term_load(p, k).start()
    mine = pl.ds(pl.multiple_of(halo * r, halo), rows)
    far = pl.ds(pl.multiple_of(rows * (1 - r), halo), halo)
    stores = []

    def put(src, dst):
        stores.append(pltpu.make_async_copy(src, dst, store.at[len(stores)]))
        stores[-1].start()

    for p in range(2):
        acc[p] = jnp.zeros(acc.shape[1:], F32)

        @pl.loop(0, count)
        def _(k):
            term_load(p, k).wait()
            row = centres[0, 0, lax.rem(k, slots), 0, k // slots] + halo * (r - 1)
            col = centres[0, 0, lax.rem(k, slots), 1, k // slots]
            top = pl.multiple_of(row // 8 * 8, 8)
            lane = pl.multiple_of(col // LANE * LANE, LANE)
            acc[p, pl.ds(top, n + 8), pl.ds(lane, n + LANE)] += shifted_out(terms[k, p].astype(F32), row - top, col - lane)

        put(acc.at[p, mine, pl.ds(halo, cols)], centre_ref.at[p, 0])
        row_buf[p] = acc[p, far, pl.ds(halo, cols)].astype(BF16)
        put(row_buf.at[p], row_ref.at[p])
        for i, at in enumerate((halo + cols, 0)):
            side_buf[i, p] = acc[p, mine, pl.ds(at, halo)].astype(BF16)
            put(side_buf.at[i, p], side_ref.at[i, p])
            corner_buf[i, p] = acc[p, far, pl.ds(at, halo)].astype(BF16)
            put(corner_buf.at[i, p], corner_ref.at[i, p])
    for copy in stores:
        copy.wait()


def scatter(centres, terms, rows, cols, halo):
    count, _, n, _ = terms.shape
    shapes = [((2, 1, rows, cols), F32), ((2, halo, cols), BF16), ((2, 2, rows, halo), BF16), ((2, 2, halo, halo), BF16)]
    return pl.pallas_call(
        functools.partial(scatter_kernel, halo),
        out_shape=tuple(jax.ShapeDtypeStruct(s, t) for s, t in shapes),
        in_specs=[pl.BlockSpec(memory_space=pltpu.SMEM), ANY],
        out_specs=(ANY,) * 4,
        scratch_shapes=[
            pltpu.VMEM(terms.shape, BF16),
            pltpu.VMEM((2, rows + halo + 8, cols + 2 * halo), F32),
        ]
        + [pltpu.VMEM(s, t) for s, t in shapes[1:]]
        + [pltpu.SemaphoreType.DMA((2, count)), pltpu.SemaphoreType.DMA((12,))],
        name="scatter",
    )(centres, terms)


def x_peer(q):
    d, _, c = axis_ids()
    return (d, q // 2, c // 2 * 2 + lax.rem(q, 2))


def plane_peer(q):
    d, r, c = axis_ids()
    return (d, r, q * 2 + lax.rem(c, 2))


def return_kernel(row_ref, side_ref, corner_ref, total_ref, row_out, side_out, corner_out, probe_out, keep_ref, got_ref, buf, line, plane, final, local, strips, xs, ps, gs, give):
    d, r, c = axis_ids()
    planes = lax.axis_size("col") // 2
    my_x = r * 2 + lax.rem(c, 2)
    my_p = c // 2
    peers = neighbours()
    line_peers = [lax.rem(my_x + t, 4) for t in range(1, 4)]
    plane_peers = [lax.rem(my_p + t, planes) for t in range(1, planes)]
    mid = keep_ref.shape[1]

    def rows_of(depth):
        return total_ref.at[:, pl.ds(pl.multiple_of(depth * mid, 8), mid)]

    load = pltpu.make_async_copy(rows_of(d), keep_ref, local.at[0])
    load.start()
    partner = (1 - d, r, c)
    meet([partner] + peers + [x_peer(q) for q in line_peers] + [plane_peer(q) for q in plane_peers])
    other = pltpu.make_async_remote_copy(rows_of(1 - d), got_ref, give[0].at[0], give[1].at[0], device_id=partner, device_id_type=MESH)
    other.start()
    wide = row_ref.shape[-1] // 2
    groups = [[] for _ in range(4)]
    for p in range(2):
        for i in range(2):
            part = (p, slice(None), pl.ds(i * wide, wide))
            groups[2 * p + i].append((row_ref.at[part], row_out.at[part], peers[0]))
            groups[2 * p + i].append((side_ref.at[i, p], side_out.at[i, p], peers[1 + i]))
            groups[2 * p + i].append((corner_ref.at[i, p], corner_out.at[i, p], peers[3 + i]))
    copies = []

    def launch(chosen):
        for s, t, peer in [m for g in chosen for m in groups[g]]:
            copies.append(remote(s, t, strips, len(copies), peer))
            copies[-1].start()

    launch(ORDER[0])
    load.wait()
    other.wait()
    half_rows, n = keep_ref.shape[1:]
    at = 0
    for p in range(2):
        for t in range(half_rows // 8):
            for h in range(n // LANE):
                place = (p, pl.ds(8 * t, 8), pl.ds(LANE * h, LANE))
                buf[at] = keep_ref[place] + got_ref[place]
                at += 1
    share = at // planes

    def piece(ref, q):
        return ref.at[pl.ds(q * share, share)]

    def send(src, dst, sems, q, me, peer):
        copy = pltpu.make_async_remote_copy(src, dst, sems[0].at[q], sems[1].at[me], device_id=peer, device_id_type=MESH)
        copy.start()
        sent.append(copy)

    def receive(dst, sems, q, peer):
        pltpu.make_async_remote_copy(dst, dst, sems[0].at[q], sems[1].at[q], device_id=peer, device_id_type=MESH).wait_recv()

    sent = []
    for q in plane_peers:
        send(piece(buf, q), plane.at[my_p], ps, q, my_p, plane_peer(q))
    launch(ORDER[1])
    for q in plane_peers:
        receive(plane.at[q], ps, q, plane_peer(q))
    total = buf[pl.ds(my_p * share, share)]
    for q in plane_peers:
        total = total + plane[q]
    line[my_x] = total
    for q in line_peers:
        send(line.at[my_x], line.at[my_x], xs, q, my_x, x_peer(q))
    launch(ORDER[2])
    for q in line_peers:
        receive(line.at[q], xs, q, x_peer(q))
    final[...] = (line[0] + line[1]) + (line[2] + line[3])
    own = pltpu.make_async_copy(final, piece(probe_out, my_p), local.at[2])
    own.start()
    for q in plane_peers:
        send(final, piece(probe_out, my_p), gs, q, my_p, plane_peer(q))
    launch(ORDER[3])
    for q in plane_peers:
        receive(piece(probe_out, q), gs, q, plane_peer(q))
    own.wait()
    for copy in sent:
        copy.wait_send()
    for copy in copies:
        copy.wait()


def send_back(row, side, corner, total):
    _, n, _ = total.shape
    chunks = n * n // (8 * LANE)
    planes = lax.axis_size("col") // 2
    share = chunks // planes
    dma = lambda n: [pltpu.SemaphoreType.DMA((n,)), pltpu.SemaphoreType.DMA((n,))]
    return pl.pallas_call(
        return_kernel_flat,
        out_shape=tuple(jax.ShapeDtypeStruct(a.shape, a.dtype) for a in (row, side, corner)) + (jax.ShapeDtypeStruct((chunks, 8, LANE), F32),),
        in_specs=[ANY] * 4,
        out_specs=(ANY,) * 4,
        scratch_shapes=[
            pltpu.VMEM((2, n // 2, n), F32),
            pltpu.VMEM((2, n // 2, n), F32),
            pltpu.VMEM((chunks, 8, LANE), F32),
            pltpu.VMEM((4, share, 8, LANE), F32),
            pltpu.VMEM((planes, share, 8, LANE), F32),
            pltpu.VMEM((share, 8, LANE), F32),
            pltpu.SemaphoreType.DMA((3,)),
        ]
        + dma(12) + dma(4) + dma(planes) + dma(planes) + dma(1),
        compiler_params=pltpu.CompilerParams(collective_id=3, has_side_effects=True),
        name=NAME,
    )(row, side, corner, total)


def return_kernel_flat(*refs):
    sems = refs[15:]
    return_kernel(*refs[:15], *[sems[i : i + 2] for i in range(0, 10, 2)])


def fold_kernel(halo, centre_ref, row_hbm, side_hbm, corner_hbm, chunks_hbm, out_ref, probe_out, sides, middle, row_ref, side_ref, corner_ref, chunks_ref, probe_ref, load, extra, store):
    _, r, _ = axis_ids()
    _, _, rows, cols = out_ref.shape
    edge = pl.ds(pl.multiple_of((rows - halo) * (1 - r), halo), halo)
    inner = pl.ds(halo, cols - 2 * halo)
    strips = [(row_hbm, row_ref), (side_hbm, side_ref), (corner_hbm, corner_ref), (chunks_hbm, chunks_ref)]
    places = []
    for p in range(2):
        places.append((out_ref.at[p, 0, edge, inner], middle.at[p]))
        for i in range(2):
            places.append((out_ref.at[p, 0, :, pl.ds(i * (cols - halo), halo)], sides.at[i, p]))
    brought = [pltpu.make_async_copy(a, b, extra.at[j]) for j, (a, b) in enumerate(strips)]
    loads = [pltpu.make_async_copy(a, b, load.at[j]) for j, (a, b) in enumerate(places)]
    stores = [pltpu.make_async_copy(b, a, store.at[j]) for j, (a, b) in enumerate(places)]
    stores.append(pltpu.make_async_copy(probe_ref, probe_out, store.at[len(places)]))
    brought[0].start()
    loads[0].start()
    brought[1].start()
    brought[2].start()
    for copy in loads[1:]:
        copy.start()
    brought[3].start()
    for copy in brought[:3]:
        copy.wait()
    for p in range(2):
        loads[3 * p].wait()
        middle[p] += row_ref[p, :, inner].astype(F32)
        stores[3 * p].start()
        for i in range(2):
            loads[3 * p + 1 + i].wait()
            sides[i, p] += side_ref[i, p].astype(F32)
            sides[i, p, edge, :] += row_ref[p, :, pl.ds(i * (cols - halo), halo)].astype(F32) + corner_ref[i, p].astype(F32)
            stores[3 * p + 1 + i].start()
    brought[3].wait()
    at = 0
    _, half_rows, n = probe_ref.shape
    for p in range(2):
        for t in range(half_rows // 8):
            for h in range(n // LANE):
                probe_ref[p, pl.ds(8 * t, 8), pl.ds(LANE * h, LANE)] = chunks_ref[at]
                at += 1
    stores[-1].start()
    for copy in stores:
        copy.wait()


def fold(centre, row, side, corner, chunks, n):
    halo = row.shape[1]
    _, _, rows, cols = centre.shape
    return pl.pallas_call(
        functools.partial(fold_kernel, halo),
        out_shape=(jax.ShapeDtypeStruct(centre.shape, F32), jax.ShapeDtypeStruct((2, n // 2, n), F32)),
        in_specs=[ANY] * 5,
        out_specs=(ANY, ANY),
        scratch_shapes=[
            pltpu.VMEM((2, 2, rows, halo), F32),
            pltpu.VMEM((2, halo, cols - 2 * halo), F32),
        ]
        + [pltpu.VMEM(a.shape, a.dtype) for a in (row, side, corner, chunks)]
        + [pltpu.VMEM((2, n // 2, n), F32)]
        + [pltpu.SemaphoreType.DMA((6,)), pltpu.SemaphoreType.DMA((4,)), pltpu.SemaphoreType.DMA((7,))],
        input_output_aliases={0: 0},
        name="fold",
    )(centre, row, side, corner, chunks)


def shards(probe, object_re, object_im, phases, centres, occupied, measured):
    n = probe.shape[1]
    _, rows, cols = object_re.shape
    mats, perm = (jnp.asarray(x) for x in constants(n))
    centres = jnp.transpose(centres, (0, 1, 3, 4, 2))
    padded, kern, frames = exchange_halo(object_re, object_im, phases, perm, measured, n // 2)
    mine, theirs = extract(centres, occupied, padded, n)
    terms, total = waves(probe, kern, mats, mine, theirs, frames)
    centre, row, side, corner = scatter(centres, terms, rows, cols, n // 2)
    row, side, corner, chunks = send_back(row, side, corner, total)
    return fold(centre, row, side, corner, chunks, n)


def solution(mesh):
    in_specs = (
        P(),
        P("depth", "row", "col"),
        P("depth", "row", "col"),
        P(),
        P("row", "col", None, None, None),
        P("row", "col", None),
        P("row", "col", None, None, None, None),
    )
    out_specs = (P(None, "depth", "row", "col"), P(None, "depth", None))
    return jax.shard_map(shards, mesh=mesh, in_specs=in_specs, out_specs=out_specs, check_vma=False)
```

```python
import functools

import jax
import jax.numpy as jnp
import numpy as np
from jax import lax
from jax.experimental import pallas as pl
from jax.experimental.pallas import tpu as pltpu
from jax.sharding import PartitionSpec as P

MESH = pl.DeviceIdType.MESH
F32 = jnp.float32
BF16 = jnp.bfloat16
ANY = pl.BlockSpec(memory_space=pl.ANY)
LANE = 128
ORDER = ((0,), (1,), (), (2,), (3,), ())
REDUCE = True
NAME = 'halo_out'


def constants(n):
    half = n // 2
    k = np.arange(half)
    parts = []
    for parity in range(2):
        turns = (np.outer(2 * k + parity, k) % n) / n
        w = np.exp(-2j * np.pi * turns) / np.sqrt(n)
        block = np.block([[w.real, -w.imag], [w.imag, w.real]])
        for matrix in (block, block.T):
            high = matrix.astype(np.float32).astype(BF16)
            low = (matrix - high.astype(np.float64)).astype(np.float32).astype(BF16)
            parts += [high, low]
    order = np.concatenate([np.arange(0, n, 2), np.arange(1, n, 2)])
    perm = np.zeros((n, n), np.float32)
    perm[np.arange(n), order] = 1.0
    return np.stack(parts), np.stack([perm, perm.T]).astype(BF16)


def axis_ids():
    return lax.axis_index("depth"), lax.axis_index("row"), lax.axis_index("col")


def meet(peers):
    barrier = pltpu.get_barrier_semaphore()
    for peer in peers:
        pl.semaphore_signal(barrier, inc=1, device_id=peer, device_id_type=MESH)
    pl.semaphore_wait(barrier, len(peers))


def remote(src, dst, sems, slot, peer):
    return pltpu.make_async_remote_copy(
        src_ref=src, dst_ref=dst, send_sem=sems[0].at[slot], recv_sem=sems[1].at[slot], device_id=peer, device_id_type=MESH
    )


def neighbours():
    d, r, c = axis_ids()
    cols = lax.axis_size("col")
    right, left = lax.rem(c + 1, cols), lax.rem(c + cols - 1, cols)
    return [(d, 1 - r, c), (d, r, right), (d, r, left), (d, 1 - r, right), (d, 1 - r, left)]


def shifted_in(x, down, right):
    rows, cols = x.shape
    turned = pltpu.roll(x.reshape(rows // 8, 8, cols), jnp.bitwise_and(8 - down, 7), 1)
    sub = lax.broadcasted_iota(jnp.int32, (rows // 8 - 1, 8, cols), 1)
    x = jnp.where(sub < 8 - down, turned[:-1], turned[1:]).reshape(rows - 8, cols)
    turned = [pltpu.roll(x[:, i : i + LANE], jnp.bitwise_and(LANE - right, LANE - 1), 1) for i in range(0, cols, LANE)]
    lanes = lax.broadcasted_iota(jnp.int32, turned[0].shape, 1)
    return jnp.concatenate([jnp.where(lanes < LANE - right, a, b) for a, b in zip(turned[:-1], turned[1:])], 1)


def shifted_out(x, down, right):
    rows, cols = x.shape
    turned = [pltpu.roll(x[:, i : i + LANE], right, 1) for i in range(0, cols, LANE)]
    lanes = lax.broadcasted_iota(jnp.int32, turned[0].shape, 1)
    none = jnp.zeros_like(turned[0])
    x = jnp.concatenate([jnp.where(lanes < right, a, b) for a, b in zip([none] + turned, turned + [none])], 1)
    cols = cols + LANE
    turned = pltpu.roll(x.reshape(rows // 8, 8, cols), down, 1)
    none = jnp.zeros((1, 8, cols), x.dtype)
    sub = lax.broadcasted_iota(jnp.int32, (rows // 8 + 1, 8, cols), 1)
    both = jnp.where(sub < down, jnp.concatenate([none, turned], 0), jnp.concatenate([turned, none], 0))
    return both.reshape(rows + 8, cols)


def split(x):
    high = x.astype(BF16)
    return high, (x - high.astype(F32)).astype(BF16)


def make_transforms(mats_ref):
    def mat(parity, transposed):
        at = parity * 4 + transposed * 2
        return mats_ref[at], mats_ref[at + 1]

    def left(z, parity, transposed, exact):
        high, low = mat(parity, transposed)
        zh, zl = split(jnp.concatenate(z, 0))
        if not exact:
            return jnp.dot(jnp.concatenate([high, high], 1), jnp.concatenate([zh, zl], 0), preferred_element_type=F32)
        out = jnp.dot(jnp.concatenate([high, low], 0), zh, preferred_element_type=F32)
        n = out.shape[0] // 2
        return out[:n] + (out[n:] + jnp.dot(high, zl, preferred_element_type=F32))

    def right(z, parity, transposed, exact):
        high, low = mat(parity, transposed)
        zh, zl = split(jnp.concatenate(z, 1))
        if not exact:
            out = jnp.dot(jnp.concatenate([zh, zl], 0), high, preferred_element_type=F32)
            n = out.shape[0] // 2
            return out[:n] + out[n:]
        out = jnp.dot(jnp.concatenate([zh, zl], 0), high, preferred_element_type=F32)
        n = out.shape[0] // 2
        return out[:n] + (out[n:] + jnp.dot(zh, low, preferred_element_type=F32))

    def halves(z):
        h = z.shape[0] // 2
        return z[:h], z[h:]

    def sides(z):
        h = z.shape[1] // 2
        return z[:, :h], z[:, h:]

    def fold(parts, parity):
        return parts[0] + parts[1] if parity == 0 else parts[0] - parts[1]

    def forward(fields, exact=True):
        outs = [[left([fold(halves(x), parity) for x in z], parity, 0, exact) for parity in range(2)] for z in fields]
        fields = [[jnp.concatenate([halves(o)[i] for o in out], 0) for i in range(2)] for out in outs]
        outs = [[right([fold(sides(x), parity) for x in z], parity, 1, exact) for parity in range(2)] for z in fields]
        return [[jnp.concatenate([sides(o)[i] for o in out], 1) for i in range(2)] for out in outs]

    def inverse(fields, exact=True):
        outs = [[left([halves(x)[parity] for x in z], parity, 1, exact) for parity in range(2)] for z in fields]
        fields = [[jnp.concatenate([fold([halves(o)[i] for o in out], q) for q in range(2)], 0) for i in range(2)] for out in outs]
        outs = [[right([sides(x)[parity] for x in z], parity, 0, exact) for parity in range(2)] for z in fields]
        return [[jnp.concatenate([fold([sides(o)[i] for o in out], q) for q in range(2)], 1) for i in range(2)] for out in outs]

    return forward, inverse


def cmul(ar, ai, br, bi):
    return ar * br - ai * bi, ar * bi + ai * br


def conj_mul(ar, ai, br, bi):
    return ar * br + ai * bi, ar * bi - ai * br


def rounded(x):
    return x.astype(BF16).astype(F32)


def halo_kernel(half, halo, phases_ref, perm_ref, re_ref, im_ref, frames_ref, pad_ref, kern_ref, ready_ref, stage, frames, phases, perm, kern, ready, send, recv, own):
    d, r, _ = axis_ids()
    _, rows, cols = re_ref.shape
    slots = frames_ref.shape[3]
    batch = half // slots
    peers = neighbours()
    everything, first, last = pl.ds(0, rows), pl.ds(0, halo), pl.ds(cols - halo, halo)
    middle, before, after = pl.ds(halo, cols), pl.ds(0, halo), pl.ds(halo + cols, halo)
    edge = pl.ds(pl.multiple_of((rows - halo) * (1 - r), halo), halo)
    far = pl.ds(pl.multiple_of(rows * r, halo), halo)
    mine = pl.ds(pl.multiple_of(halo * r, halo), rows)
    meet(peers)
    moves = [
        (edge, pl.ds(0, cols), far, middle),
        (everything, last, mine, before),
        (everything, first, mine, after),
        (edge, last, far, before),
        (edge, first, far, after),
    ]
    copies = []
    for p, src in enumerate((re_ref, im_ref)):
        for i, (sr, sc, dr, dc) in enumerate(moves):
            copies.append(remote(src.at[0, sr, sc], pad_ref.at[p, dr, dc], (send, recv), p * 5 + i, peers[i]))
            copies[-1].start()
    sources = [
        (phases_ref, phases),
        (perm_ref, perm),
        (frames_ref.at[0, 0, pl.ds(d * batch, batch)], frames),
        (re_ref.at[0], stage.at[0]),
        (im_ref.at[0], stage.at[1]),
    ]
    targets = [
        (kern, kern_ref),
        (ready, ready_ref),
        (stage.at[0], pad_ref.at[0, mine, middle]),
        (stage.at[1], pad_ref.at[1, mine, middle]),
    ]
    loads = [pltpu.make_async_copy(a, b, own.at[i]) for i, (a, b) in enumerate(sources)]
    stores = [pltpu.make_async_copy(a, b, own.at[5 + i]) for i, (a, b) in enumerate(targets)]
    for load in loads:
        load.start()
    loads[0].wait()
    loads[1].wait()
    kern[0] = reorder(jnp.cos(phases[...]), perm, True)
    kern[1] = reorder(jnp.sin(phases[...]), perm, True)
    stores[0].start()
    for load, store in zip(loads[3:], stores[2:]):
        load.wait()
        store.start()
    loads[2].wait()

    @pl.loop(0, half)
    def _(k):
        ready[k] = reorder(frames[k // slots, lax.rem(k, slots)], perm, True)

    stores[1].start()
    for store in stores:
        store.wait()
    for copy in copies:
        copy.wait()


def exchange_halo(object_re, object_im, phases, perm, measured, halo):
    _, rows, cols = object_re.shape
    batches, slots, n = measured.shape[2:5]
    half = batches * slots // 2
    dma = pltpu.SemaphoreType.DMA
    return pl.pallas_call(
        functools.partial(halo_kernel, half, halo),
        out_shape=(
            jax.ShapeDtypeStruct((2, rows + halo, cols + 2 * halo), BF16),
            jax.ShapeDtypeStruct((2, n, n), F32),
            jax.ShapeDtypeStruct((half, n, n), F32),
        ),
        in_specs=[ANY] * 5,
        out_specs=(ANY,) * 3,
        scratch_shapes=[
            pltpu.VMEM((2, rows, cols), BF16),
            pltpu.VMEM((half // slots, slots, n, n), F32),
            pltpu.VMEM(phases.shape, F32),
            pltpu.VMEM(perm.shape, BF16),
            pltpu.VMEM((2, n, n), F32),
            pltpu.VMEM((half, n, n), F32),
            dma((10,)), dma((10,)), dma((9,)),
        ],
        compiler_params=pltpu.CompilerParams(collective_id=0, has_side_effects=True),
        name="halo_in",
    )(phases, perm, object_re, object_im, measured)


def extract_kernel(halo, centres, occupied, pad_ref, mine_ref, theirs_ref, pieces, wide, load, store, done):
    d, r, _ = axis_ids()
    count = pieces.shape[0]
    half = count // 2
    n = done.shape[-1]
    tall = n + 16
    rows_all = pad_ref.shape[1]
    slots = centres.shape[2]

    def place(k):
        at = jnp.where(k < half, (1 - d) * half + k, d * half + k - half)
        batch, slot = at // slots, lax.rem(at, slots)
        row = centres[0, 0, slot, 0, batch] + halo * (r - 1)
        col = centres[0, 0, slot, 1, batch]
        base = pl.multiple_of(jnp.minimum(row // 16 * 16, rows_all - tall), 16)
        lane = pl.multiple_of(col // LANE * LANE, LANE)
        return base, lane, row - base, col - lane, slot < occupied[0, 0, batch]

    def piece_load(k):
        base, lane, _, _, _ = place(k)
        return pltpu.make_async_copy(pad_ref.at[:, pl.ds(base, tall), pl.ds(lane, n + LANE)], pieces.at[k], load.at[k])

    @pl.loop(0, count)
    def _(k):
        piece_load(k).start()

    def cut(k):
        piece_load(k).wait()
        _, _, down, right, live = place(k)
        skip = pl.multiple_of(down // 8 * 8, 8)
        for p in range(2):
            wide[p, pl.ds(0, tall), :] = pieces[k, p].astype(F32)
            window = shifted_in(wide[p, pl.ds(skip, n + 8), :], down - skip, right)
            done[k, p] = jnp.where(live, window, 0.0).astype(BF16)

    for part, out in enumerate((theirs_ref, mine_ref)):
        @pl.loop(0, half)
        def _(k):
            cut(part * half + k)
            pltpu.make_async_copy(done.at[part * half + k], out.at[k], store.at[part * half + k]).start()

    for part, out in enumerate((theirs_ref, mine_ref)):
        for k in range(half):
            pltpu.make_async_copy(done.at[part * half + k], out.at[k], store.at[part * half + k]).wait()


def extract(centres, occupied, padded, n):
    count = occupied.shape[2] * centres.shape[2]
    half = count // 2
    shape = jax.ShapeDtypeStruct((half, 2, n, n), BF16)
    smem = pl.BlockSpec(memory_space=pltpu.SMEM)
    return pl.pallas_call(
        functools.partial(extract_kernel, n // 2),
        out_shape=(shape, shape),
        in_specs=[smem, smem, ANY],
        out_specs=(ANY, ANY),
        scratch_shapes=[
            pltpu.VMEM((count, 2, n + 16, n + LANE), BF16),
            pltpu.VMEM((2, n + 24, n + LANE), F32),
            pltpu.SemaphoreType.DMA((count,)),
            pltpu.SemaphoreType.DMA((count,)),
            pltpu.VMEM((count, 2, n, n), BF16),
        ],
        name="extract",
    )(centres, occupied, padded)


def reorder(x, perm_ref, both):
    high, low = split(x)
    if both:
        high = jnp.dot(perm_ref[0], high, preferred_element_type=F32).astype(BF16)
        low = jnp.dot(perm_ref[0], low, preferred_element_type=F32).astype(BF16)
    return jnp.dot(high, perm_ref[1], preferred_element_type=F32) + jnp.dot(low, perm_ref[1], preferred_element_type=F32)


def wave_kernel(
    half, probe_hbm, kern_hbm, mats_hbm, mine_ref, theirs_ref, frames_ref,
    terms_ref, total_ref,
    windows, frames, probe_ref, kern, mats_ref, fixed, grads, total, own_sem, frame_sem, swap_send, swap_recv, term_send, term_recv, term_own, total_sem,
):
    d, r, c = axis_ids()
    n = probe_ref.shape[1]
    steady = [pltpu.make_async_copy(a, b, fixed.at[i]) for i, (a, b) in enumerate([(mats_hbm, mats_ref), (probe_hbm, probe_ref), (kern_hbm, kern)])]
    for copy in steady:
        copy.start()
    partner = (1 - d, r, c)

    def own_copy(k):
        return pltpu.make_async_copy(mine_ref.at[k], windows.at[d, k], own_sem.at[k])

    def frame_copy(k):
        return pltpu.make_async_copy(frames_ref.at[k], frames.at[k], frame_sem.at[k])

    def window_copy(k):
        return remote(theirs_ref.at[k], windows.at[d, k], (swap_send, swap_recv), k, partner)

    def term_copies(k):
        there = terms_ref.at[d * half + k]
        return (
            remote(grads.at[1 - d, k], there, (term_send, term_recv), k, partner),
            pltpu.make_async_copy(grads.at[d, k], there, term_own.at[k]),
        )

    @pl.loop(0, half)
    def _(k):
        own_copy(k).start()

    meet([partner])

    @pl.loop(0, half)
    def _(k):
        window_copy(k).start()
        frame_copy(k).start()

    total[...] = jnp.zeros_like(total)
    forward, inverse = make_transforms(mats_ref)
    for copy in steady:
        copy.wait()

    group = 2

    @pl.loop(0, half // group)
    def _(step):
        ks = [step * group + i for i in range(group)]

        def window(s, k):
            return [windows[s, k, p].astype(F32) for p in range(2)]

        for k in ks:
            own_copy(k).wait()
            frame_copy(k).wait()
            window_copy(k).wait()
        waves = forward([cmul(probe_ref[0], probe_ref[1], *window(0, k)) for k in ks])
        waves = inverse([cmul(fr, fi, kern[0], kern[1]) for fr, fi in waves])
        waves = [(rounded(pr), rounded(pi)) for pr, pi in waves]
        fields = forward([cmul(*wave, *window(1, k)) for wave, k in zip(waves, ks)])
        misfits = [fr * fr + fi * fi - frames[k] for (fr, fi), k in zip(fields, ks)]
        fields = inverse([(m * fr, m * fi) for (fr, fi), m in zip(fields, misfits)], False)
        for k, wave, field in zip(ks, waves, fields):
            gr, gi = conj_mul(*wave, *field)
            grads[1, k, 0] = gr.astype(BF16)
            grads[1, k, 1] = gi.astype(BF16)
        fields = forward([conj_mul(*window(1, k), *field) for k, field in zip(ks, fields)], False)
        fields = inverse([conj_mul(kern[0], kern[1], *field) for field in fields], False)
        fields = [(rounded(xr), rounded(xi)) for xr, xi in fields]
        for k, field in zip(ks, fields):
            gr, gi = conj_mul(probe_ref[0], probe_ref[1], *field)
            grads[0, k, 0] = gr.astype(BF16)
            grads[0, k, 1] = gi.astype(BF16)
            lr, li = conj_mul(*window(0, k), *field)
            total[0] += lr
            total[1] += li
            for copy in term_copies(k):
                copy.start()

    last_copy = pltpu.make_async_copy(total, total_ref, total_sem)
    last_copy.start()

    @pl.loop(0, half)
    def _(k):
        for copy in term_copies(k):
            copy.wait()

    last_copy.wait()


def waves(probe, kern, mats, mine, theirs, frames):
    half, _, n, _ = mine.shape
    dma = pltpu.SemaphoreType.DMA
    return pl.pallas_call(
        functools.partial(wave_kernel, half),
        out_shape=(
            jax.ShapeDtypeStruct((2 * half, 2, n, n), BF16),
            jax.ShapeDtypeStruct((2, n, n), F32),
        ),
        in_specs=[ANY] * 6,
        out_specs=(ANY, ANY),
        scratch_shapes=[
            pltpu.VMEM((2, half, 2, n, n), BF16),
            pltpu.VMEM((half, n, n), F32),
            pltpu.VMEM(probe.shape, F32),
            pltpu.VMEM(kern.shape, F32),
            pltpu.VMEM(mats.shape, BF16),
            dma((3,)),
            pltpu.VMEM((2, half, 2, n, n), BF16),
            pltpu.VMEM((2, n, n), F32),
        ]
        + [dma((half,))] * 7 + [dma(())],
        compiler_params=pltpu.CompilerParams(collective_id=1, has_side_effects=True),
        name="waves",
    )(probe, kern, mats, mine, theirs, frames)


def scatter_kernel(halo, centres, terms_ref, centre_ref, row_ref, side_ref, corner_ref, terms, acc, row_buf, side_buf, corner_buf, load, store):
    _, r, _ = axis_ids()
    count, _, n, _ = terms.shape
    _, _, rows, cols = centre_ref.shape
    slots = centres.shape[2]

    def term_load(p, k):
        return pltpu.make_async_copy(terms_ref.at[k, p], terms.at[k, p], load.at[p, k])

    for p in range(2):
        for k in range(count):
            term_load(p, k).start()
    mine = pl.ds(pl.multiple_of(halo * r, halo), rows)
    far = pl.ds(pl.multiple_of(rows * (1 - r), halo), halo)
    stores = []

    def put(src, dst):
        stores.append(pltpu.make_async_copy(src, dst, store.at[len(stores)]))
        stores[-1].start()

    for p in range(2):
        acc[p] = jnp.zeros(acc.shape[1:], F32)

        @pl.loop(0, count)
        def _(k):
            term_load(p, k).wait()
            row = centres[0, 0, lax.rem(k, slots), 0, k // slots] + halo * (r - 1)
            col = centres[0, 0, lax.rem(k, slots), 1, k // slots]
            top = pl.multiple_of(row // 8 * 8, 8)
            lane = pl.multiple_of(col // LANE * LANE, LANE)
            acc[p, pl.ds(top, n + 8), pl.ds(lane, n + LANE)] += shifted_out(terms[k, p].astype(F32), row - top, col - lane)

        put(acc.at[p, mine, pl.ds(halo, cols)], centre_ref.at[p, 0])
        row_buf[p] = acc[p, far, pl.ds(halo, cols)].astype(BF16)
        put(row_buf.at[p], row_ref.at[p])
        for i, at in enumerate((halo + cols, 0)):
            side_buf[i, p] = acc[p, mine, pl.ds(at, halo)].astype(BF16)
            put(side_buf.at[i, p], side_ref.at[i, p])
            corner_buf[i, p] = acc[p, far, pl.ds(at, halo)].astype(BF16)
            put(corner_buf.at[i, p], corner_ref.at[i, p])
    for copy in stores:
        copy.wait()


def scatter(centres, terms, rows, cols, halo):
    count, _, n, _ = terms.shape
    shapes = [((2, 1, rows, cols), F32), ((2, halo, cols), BF16), ((2, 2, rows, halo), BF16), ((2, 2, halo, halo), BF16)]
    return pl.pallas_call(
        functools.partial(scatter_kernel, halo),
        out_shape=tuple(jax.ShapeDtypeStruct(s, t) for s, t in shapes),
        in_specs=[pl.BlockSpec(memory_space=pltpu.SMEM), ANY],
        out_specs=(ANY,) * 4,
        scratch_shapes=[
            pltpu.VMEM(terms.shape, BF16),
            pltpu.VMEM((2, rows + halo + 8, cols + 2 * halo), F32),
        ]
        + [pltpu.VMEM(s, t) for s, t in shapes[1:]]
        + [pltpu.SemaphoreType.DMA((2, count)), pltpu.SemaphoreType.DMA((12,))],
        name="scatter",
    )(centres, terms)


def x_peer(q):
    d, _, c = axis_ids()
    return (d, q // 2, c // 2 * 2 + lax.rem(q, 2))


def y_peer(q):
    d, r, c = axis_ids()
    return (d, r, c // 8 * 8 + q * 2 + lax.rem(c, 2))


def z_peer(q):
    d, r, c = axis_ids()
    return (d, r, q * 8 + lax.rem(c, 8))


def return_kernel(row_ref, side_ref, corner_ref, total_ref, row_out, side_out, corner_out, probe_out, keep_ref, got_ref, buf, ys_in, y_sum, zs_in, x_in, z_all, local, strips, ys, zs, xs, zg, yg, give):
    d, r, c = axis_ids()
    my_x = r * 2 + lax.rem(c, 2)
    my_y, my_z = lax.rem(c // 2, 4), c // 8
    peers = neighbours()

    def others(me):
        return [lax.rem(me + t, 4) for t in range(1, 4)]

    mid = keep_ref.shape[1]

    def rows_of(depth):
        return total_ref.at[:, pl.ds(pl.multiple_of(depth * mid, 8), mid)]

    load = pltpu.make_async_copy(rows_of(d), keep_ref, local.at[0])
    load.start()
    partner = (1 - d, r, c)
    meet([partner] + peers + [y_peer(q) for q in others(my_y)] + [z_peer(q) for q in others(my_z)])
    other = pltpu.make_async_remote_copy(rows_of(1 - d), got_ref, give[0].at[0], give[1].at[0], device_id=partner, device_id_type=MESH)
    other.start()
    wide = row_ref.shape[-1] // 2
    groups = [[] for _ in range(4)]
    for p in range(2):
        for i in range(2):
            part = (p, slice(None), pl.ds(i * wide, wide))
            groups[2 * p + i].append((row_ref.at[part], row_out.at[part], peers[0]))
            groups[2 * p + i].append((side_ref.at[i, p], side_out.at[i, p], peers[1 + i]))
            groups[2 * p + i].append((corner_ref.at[i, p], corner_out.at[i, p], peers[3 + i]))
    copies = []

    def launch(chosen):
        for s, t, peer in [m for g in chosen for m in groups[g]]:
            copies.append(remote(s, t, strips, len(copies), peer))
            copies[-1].start()

    launch(ORDER[0])
    load.wait()
    other.wait()
    half_rows, n = keep_ref.shape[1:]
    at = 0
    for p in range(2):
        for t in range(half_rows // 8):
            for h in range(n // LANE):
                place = (p, pl.ds(8 * t, 8), pl.ds(LANE * h, LANE))
                buf[at] = keep_ref[place] + got_ref[place]
                at += 1

    def quarter(ref, q):
        size = ref.shape[0] // 4
        return ref.at[pl.ds(q * size, size)]

    sent = []

    def send(src, dst, sems, q, me, peer):
        copy = pltpu.make_async_remote_copy(src, dst, sems[0].at[q], sems[1].at[me], device_id=peer, device_id_type=MESH)
        copy.start()
        sent.append(copy)

    def receive(dst, sems, q, peer):
        pltpu.make_async_remote_copy(dst, dst, sems[0].at[q], sems[1].at[q], device_id=peer, device_id_type=MESH).wait_recv()

    for q in others(my_y):
        send(quarter(buf, q), ys_in.at[my_y], ys, q, my_y, y_peer(q))
    launch(ORDER[1])
    part = quarter(buf, my_y)[...]
    for q in others(my_y):
        receive(ys_in.at[q], ys, q, y_peer(q))
        part = part + ys_in[q]
    y_sum[...] = part
    for q in others(my_z):
        send(quarter(y_sum, q), zs_in.at[my_z], zs, q, my_z, z_peer(q))
    launch(ORDER[2])
    part = quarter(y_sum, my_z)[...]
    for q in others(my_z):
        receive(zs_in.at[q], zs, q, z_peer(q))
        part = part + zs_in[q]
    x_in[my_x] = part
    for q in others(my_x):
        send(x_in.at[my_x], x_in.at[my_x], xs, q, my_x, x_peer(q))
    launch(ORDER[3])
    for q in others(my_x):
        receive(x_in.at[q], xs, q, x_peer(q))
    z_all[my_z] = (x_in[0] + x_in[1]) + (x_in[2] + x_in[3])
    for q in others(my_z):
        send(z_all.at[my_z], z_all.at[my_z], zg, q, my_z, z_peer(q))
    launch(ORDER[4])
    for q in others(my_z):
        receive(z_all.at[q], zg, q, z_peer(q))
    own = pltpu.make_async_copy(z_all, probe_out.at[my_y], local.at[1])
    own.start()
    for q in others(my_y):
        send(z_all, probe_out.at[my_y], yg, q, my_y, y_peer(q))
    launch(ORDER[5])
    for q in others(my_y):
        receive(probe_out.at[q], yg, q, y_peer(q))
    own.wait()
    for copy in sent:
        copy.wait_send()
    for copy in copies:
        copy.wait()


def send_back(row, side, corner, total):
    _, n, _ = total.shape
    share = n * n // (64 * 8 * LANE)
    dma = lambda n: [pltpu.SemaphoreType.DMA((n,)), pltpu.SemaphoreType.DMA((n,))]
    chunk = lambda *lead: pltpu.VMEM(lead + (8, LANE), F32)
    return pl.pallas_call(
        return_kernel_flat,
        out_shape=tuple(jax.ShapeDtypeStruct(a.shape, a.dtype) for a in (row, side, corner)) + (jax.ShapeDtypeStruct((4, 4, 4 * share, 8, LANE), F32),),
        in_specs=[ANY] * 4,
        out_specs=(ANY,) * 4,
        scratch_shapes=[
            pltpu.VMEM((2, n // 2, n), F32),
            pltpu.VMEM((2, n // 2, n), F32),
            chunk(64 * share),
            chunk(4, 16 * share),
            chunk(16 * share),
            chunk(4, 4 * share),
            chunk(4, 4 * share),
            chunk(4, 4 * share),
            pltpu.SemaphoreType.DMA((2,)),
        ]
        + dma(12) + dma(4) * 5 + dma(1),
        compiler_params=pltpu.CompilerParams(collective_id=3, has_side_effects=True),
        name=NAME,
    )(row, side, corner, total)


def return_kernel_flat(*refs):
    sems = refs[17:]
    return_kernel(*refs[:17], *[sems[i : i + 2] for i in range(0, 14, 2)])


def fold_kernel(halo, centre_ref, row_hbm, side_hbm, corner_hbm, chunks_hbm, out_ref, probe_out, sides, middle, row_ref, side_ref, corner_ref, chunks_ref, probe_ref, load, extra, store):
    _, r, _ = axis_ids()
    _, _, rows, cols = out_ref.shape
    edge = pl.ds(pl.multiple_of((rows - halo) * (1 - r), halo), halo)
    inner = pl.ds(halo, cols - 2 * halo)
    strips = [(row_hbm, row_ref), (side_hbm, side_ref), (corner_hbm, corner_ref), (chunks_hbm, chunks_ref)]
    places = []
    for p in range(2):
        places.append((out_ref.at[p, 0, edge, inner], middle.at[p]))
        for i in range(2):
            places.append((out_ref.at[p, 0, :, pl.ds(i * (cols - halo), halo)], sides.at[i, p]))
    brought = [pltpu.make_async_copy(a, b, extra.at[j]) for j, (a, b) in enumerate(strips)]
    loads = [pltpu.make_async_copy(a, b, load.at[j]) for j, (a, b) in enumerate(places)]
    stores = [pltpu.make_async_copy(b, a, store.at[j]) for j, (a, b) in enumerate(places)]
    stores.append(pltpu.make_async_copy(probe_ref, probe_out, store.at[len(places)]))
    brought[0].start()
    loads[0].start()
    brought[1].start()
    brought[2].start()
    for copy in loads[1:]:
        copy.start()
    brought[3].start()
    for copy in brought[:3]:
        copy.wait()
    for p in range(2):
        loads[3 * p].wait()
        middle[p] += row_ref[p, :, inner].astype(F32)
        stores[3 * p].start()
        for i in range(2):
            loads[3 * p + 1 + i].wait()
            sides[i, p] += side_ref[i, p].astype(F32)
            sides[i, p, edge, :] += row_ref[p, :, pl.ds(i * (cols - halo), halo)].astype(F32) + corner_ref[i, p].astype(F32)
            stores[3 * p + 1 + i].start()
    brought[3].wait()
    at = 0
    _, half_rows, n = probe_ref.shape
    for p in range(2):
        for t in range(half_rows // 8):
            for h in range(n // LANE):
                probe_ref[p, pl.ds(8 * t, 8), pl.ds(LANE * h, LANE)] = chunks_ref[at // 16, at // 4 % 4, at % 4]
                at += 1
    stores[-1].start()
    for copy in stores:
        copy.wait()


def fold(centre, row, side, corner, chunks, n):
    halo = row.shape[1]
    _, _, rows, cols = centre.shape
    return pl.pallas_call(
        functools.partial(fold_kernel, halo),
        out_shape=(jax.ShapeDtypeStruct(centre.shape, F32), jax.ShapeDtypeStruct((2, n // 2, n), F32)),
        in_specs=[ANY] * 5,
        out_specs=(ANY, ANY),
        scratch_shapes=[
            pltpu.VMEM((2, 2, rows, halo), F32),
            pltpu.VMEM((2, halo, cols - 2 * halo), F32),
        ]
        + [pltpu.VMEM(a.shape, a.dtype) for a in (row, side, corner, chunks)]
        + [pltpu.VMEM((2, n // 2, n), F32)]
        + [pltpu.SemaphoreType.DMA((6,)), pltpu.SemaphoreType.DMA((4,)), pltpu.SemaphoreType.DMA((7,))],
        input_output_aliases={0: 0},
        name="fold",
    )(centre, row, side, corner, chunks)


def shards(probe, object_re, object_im, phases, centres, occupied, measured):
    n = probe.shape[1]
    _, rows, cols = object_re.shape
    mats, perm = (jnp.asarray(x) for x in constants(n))
    centres = jnp.transpose(centres, (0, 1, 3, 4, 2))
    padded, kern, frames = exchange_halo(object_re, object_im, phases, perm, measured, n // 2)
    mine, theirs = extract(centres, occupied, padded, n)
    terms, total = waves(probe, kern, mats, mine, theirs, frames)
    centre, row, side, corner = scatter(centres, terms, rows, cols, n // 2)
    row, side, corner, chunks = send_back(row, side, corner, total)
    return fold(centre, row, side, corner, chunks, n)


def solution(mesh):
    in_specs = (
        P(),
        P("depth", "row", "col"),
        P("depth", "row", "col"),
        P(),
        P("row", "col", None, None, None),
        P("row", "col", None),
        P("row", "col", None, None, None, None),
    )
    out_specs = (P(None, "depth", "row", "col"), P(None, "depth", None))
    return jax.shard_map(shards, mesh=mesh, in_specs=in_specs, out_specs=out_specs, check_vma=False)
```

```python
import functools

import jax
import jax.numpy as jnp
import numpy as np
from jax import lax
from jax.experimental import pallas as pl
from jax.experimental.pallas import tpu as pltpu
from jax.sharding import PartitionSpec as P

MESH = pl.DeviceIdType.MESH
F32 = jnp.float32
BF16 = jnp.bfloat16
ANY = pl.BlockSpec(memory_space=pl.ANY)
LANE = 128
ORDER = ((0,), (1,), (), (2,), (3,), ())
REDUCE = True
NAME = 'halo_out'


def constants(n):
    half = n // 2
    k = np.arange(half)
    parts = []
    for parity in range(2):
        turns = (np.outer(2 * k + parity, k) % n) / n
        w = np.exp(-2j * np.pi * turns) / np.sqrt(n)
        block = np.block([[w.real, -w.imag], [w.imag, w.real]])
        for matrix in (block, block.T):
            high = matrix.astype(np.float32).astype(BF16)
            low = (matrix - high.astype(np.float64)).astype(np.float32).astype(BF16)
            parts += [high, low]
    order = np.concatenate([np.arange(0, n, 2), np.arange(1, n, 2)])
    perm = np.zeros((n, n), np.float32)
    perm[np.arange(n), order] = 1.0
    return np.stack(parts), np.stack([perm, perm.T]).astype(BF16)


def axis_ids():
    return lax.axis_index("depth"), lax.axis_index("row"), lax.axis_index("col")


def meet(peers):
    barrier = pltpu.get_barrier_semaphore()
    for peer in peers:
        pl.semaphore_signal(barrier, inc=1, device_id=peer, device_id_type=MESH)
    pl.semaphore_wait(barrier, len(peers))


def remote(src, dst, sems, slot, peer):
    return pltpu.make_async_remote_copy(
        src_ref=src, dst_ref=dst, send_sem=sems[0].at[slot], recv_sem=sems[1].at[slot], device_id=peer, device_id_type=MESH
    )


def neighbours():
    d, r, c = axis_ids()
    cols = lax.axis_size("col")
    right, left = lax.rem(c + 1, cols), lax.rem(c + cols - 1, cols)
    return [(d, 1 - r, c), (d, r, right), (d, r, left), (d, 1 - r, right), (d, 1 - r, left)]


def shifted_in(x, down, right):
    rows, cols = x.shape
    turned = pltpu.roll(x.reshape(rows // 8, 8, cols), jnp.bitwise_and(8 - down, 7), 1)
    sub = lax.broadcasted_iota(jnp.int32, (rows // 8 - 1, 8, cols), 1)
    x = jnp.where(sub < 8 - down, turned[:-1], turned[1:]).reshape(rows - 8, cols)
    turned = [pltpu.roll(x[:, i : i + LANE], jnp.bitwise_and(LANE - right, LANE - 1), 1) for i in range(0, cols, LANE)]
    lanes = lax.broadcasted_iota(jnp.int32, turned[0].shape, 1)
    return jnp.concatenate([jnp.where(lanes < LANE - right, a, b) for a, b in zip(turned[:-1], turned[1:])], 1)


def shifted_out(x, down, right):
    rows, cols = x.shape
    turned = [pltpu.roll(x[:, i : i + LANE], right, 1) for i in range(0, cols, LANE)]
    lanes = lax.broadcasted_iota(jnp.int32, turned[0].shape, 1)
    none = jnp.zeros_like(turned[0])
    x = jnp.concatenate([jnp.where(lanes < right, a, b) for a, b in zip([none] + turned, turned + [none])], 1)
    cols = cols + LANE
    turned = pltpu.roll(x.reshape(rows // 8, 8, cols), down, 1)
    none = jnp.zeros((1, 8, cols), x.dtype)
    sub = lax.broadcasted_iota(jnp.int32, (rows // 8 + 1, 8, cols), 1)
    both = jnp.where(sub < down, jnp.concatenate([none, turned], 0), jnp.concatenate([turned, none], 0))
    return both.reshape(rows + 8, cols)


def split(x):
    high = x.astype(BF16)
    return high, (x - high.astype(F32)).astype(BF16)


def make_transforms(mats_ref):
    def mat(parity, transposed):
        at = parity * 4 + transposed * 2
        return mats_ref[at], mats_ref[at + 1]

    def left(z, parity, transposed, exact):
        high, low = mat(parity, transposed)
        zh, zl = split(jnp.concatenate(z, 0))
        if not exact:
            return jnp.dot(jnp.concatenate([high, high], 1), jnp.concatenate([zh, zl], 0), preferred_element_type=F32)
        out = jnp.dot(jnp.concatenate([high, low], 0), zh, preferred_element_type=F32)
        n = out.shape[0] // 2
        return out[:n] + (out[n:] + jnp.dot(high, zl, preferred_element_type=F32))

    def right(z, parity, transposed, exact):
        high, low = mat(parity, transposed)
        zh, zl = split(jnp.concatenate(z, 1))
        if not exact:
            out = jnp.dot(jnp.concatenate([zh, zl], 0), high, preferred_element_type=F32)
            n = out.shape[0] // 2
            return out[:n] + out[n:]
        out = jnp.dot(jnp.concatenate([zh, zl], 0), high, preferred_element_type=F32)
        n = out.shape[0] // 2
        return out[:n] + (out[n:] + jnp.dot(zh, low, preferred_element_type=F32))

    def halves(z):
        h = z.shape[0] // 2
        return z[:h], z[h:]

    def sides(z):
        h = z.shape[1] // 2
        return z[:, :h], z[:, h:]

    def fold(parts, parity):
        return parts[0] + parts[1] if parity == 0 else parts[0] - parts[1]

    def forward(fields, exact=True):
        outs = [[left([fold(halves(x), parity) for x in z], parity, 0, exact) for parity in range(2)] for z in fields]
        fields = [[jnp.concatenate([halves(o)[i] for o in out], 0) for i in range(2)] for out in outs]
        outs = [[right([fold(sides(x), parity) for x in z], parity, 1, exact) for parity in range(2)] for z in fields]
        return [[jnp.concatenate([sides(o)[i] for o in out], 1) for i in range(2)] for out in outs]

    def inverse(fields, exact=True):
        outs = [[left([halves(x)[parity] for x in z], parity, 1, exact) for parity in range(2)] for z in fields]
        fields = [[jnp.concatenate([fold([halves(o)[i] for o in out], q) for q in range(2)], 0) for i in range(2)] for out in outs]
        outs = [[right([sides(x)[parity] for x in z], parity, 0, exact) for parity in range(2)] for z in fields]
        return [[jnp.concatenate([fold([sides(o)[i] for o in out], q) for q in range(2)], 1) for i in range(2)] for out in outs]

    return forward, inverse


def cmul(ar, ai, br, bi):
    return ar * br - ai * bi, ar * bi + ai * br


def conj_mul(ar, ai, br, bi):
    return ar * br + ai * bi, ar * bi - ai * br


def rounded(x):
    return x.astype(BF16).astype(F32)


def halo_kernel(half, halo, phases_ref, perm_ref, re_ref, im_ref, frames_ref, pad_ref, kern_ref, ready_ref, stage, frames, phases, perm, kern, ready, send, recv, own):
    d, r, _ = axis_ids()
    _, rows, cols = re_ref.shape
    slots = frames_ref.shape[3]
    batch = half // slots
    peers = neighbours()
    everything, first, last = pl.ds(0, rows), pl.ds(0, halo), pl.ds(cols - halo, halo)
    middle, before, after = pl.ds(halo, cols), pl.ds(0, halo), pl.ds(halo + cols, halo)
    edge = pl.ds(pl.multiple_of((rows - halo) * (1 - r), halo), halo)
    far = pl.ds(pl.multiple_of(rows * r, halo), halo)
    mine = pl.ds(pl.multiple_of(halo * r, halo), rows)
    meet(peers)
    moves = [
        (edge, pl.ds(0, cols), far, middle),
        (everything, last, mine, before),
        (everything, first, mine, after),
        (edge, last, far, before),
        (edge, first, far, after),
    ]
    copies = []
    for p, src in enumerate((re_ref, im_ref)):
        for i, (sr, sc, dr, dc) in enumerate(moves):
            copies.append(remote(src.at[0, sr, sc], pad_ref.at[p, dr, dc], (send, recv), p * 5 + i, peers[i]))
            copies[-1].start()
    sources = [
        (phases_ref, phases),
        (perm_ref, perm),
        (frames_ref.at[0, 0, pl.ds(d * batch, batch)], frames),
        (re_ref.at[0], stage.at[0]),
        (im_ref.at[0], stage.at[1]),
    ]
    targets = [
        (kern, kern_ref),
        (ready, ready_ref),
        (stage.at[0], pad_ref.at[0, mine, middle]),
        (stage.at[1], pad_ref.at[1, mine, middle]),
    ]
    loads = [pltpu.make_async_copy(a, b, own.at[i]) for i, (a, b) in enumerate(sources)]
    stores = [pltpu.make_async_copy(a, b, own.at[5 + i]) for i, (a, b) in enumerate(targets)]
    for load in loads:
        load.start()
    loads[0].wait()
    loads[1].wait()
    kern[0] = reorder(jnp.cos(phases[...]), perm, True)
    kern[1] = reorder(jnp.sin(phases[...]), perm, True)
    stores[0].start()
    for load, store in zip(loads[3:], stores[2:]):
        load.wait()
        store.start()
    loads[2].wait()

    @pl.loop(0, half)
    def _(k):
        ready[k] = reorder(frames[k // slots, lax.rem(k, slots)], perm, True)

    stores[1].start()
    for store in stores:
        store.wait()
    for copy in copies:
        copy.wait()


def exchange_halo(object_re, object_im, phases, perm, measured, halo):
    _, rows, cols = object_re.shape
    batches, slots, n = measured.shape[2:5]
    half = batches * slots // 2
    dma = pltpu.SemaphoreType.DMA
    return pl.pallas_call(
        functools.partial(halo_kernel, half, halo),
        out_shape=(
            jax.ShapeDtypeStruct((2, rows + halo, cols + 2 * halo), BF16),
            jax.ShapeDtypeStruct((2, n, n), F32),
            jax.ShapeDtypeStruct((half, n, n), F32),
        ),
        in_specs=[ANY] * 5,
        out_specs=(ANY,) * 3,
        scratch_shapes=[
            pltpu.VMEM((2, rows, cols), BF16),
            pltpu.VMEM((half // slots, slots, n, n), F32),
            pltpu.VMEM(phases.shape, F32),
            pltpu.VMEM(perm.shape, BF16),
            pltpu.VMEM((2, n, n), F32),
            pltpu.VMEM((half, n, n), F32),
            dma((10,)), dma((10,)), dma((9,)),
        ],
        compiler_params=pltpu.CompilerParams(collective_id=0, has_side_effects=True),
        name="halo_in",
    )(phases, perm, object_re, object_im, measured)


def extract_kernel(halo, centres, occupied, pad_ref, mine_ref, theirs_ref, pieces, wide, load, store, done):
    d, r, _ = axis_ids()
    count = pieces.shape[0]
    half = count // 2
    n = done.shape[-1]
    tall = n + 16
    rows_all = pad_ref.shape[1]
    slots = centres.shape[2]

    def place(k):
        at = jnp.where(k < half, (1 - d) * half + k, d * half + k - half)
        batch, slot = at // slots, lax.rem(at, slots)
        row = centres[0, 0, slot, 0, batch] + halo * (r - 1)
        col = centres[0, 0, slot, 1, batch]
        base = pl.multiple_of(jnp.minimum(row // 16 * 16, rows_all - tall), 16)
        lane = pl.multiple_of(col // LANE * LANE, LANE)
        return base, lane, row - base, col - lane, slot < occupied[0, 0, batch]

    def piece_load(k):
        base, lane, _, _, _ = place(k)
        return pltpu.make_async_copy(pad_ref.at[:, pl.ds(base, tall), pl.ds(lane, n + LANE)], pieces.at[k], load.at[k])

    @pl.loop(0, count)
    def _(k):
        piece_load(k).start()

    def cut(k):
        piece_load(k).wait()
        _, _, down, right, live = place(k)
        skip = pl.multiple_of(down // 8 * 8, 8)
        for p in range(2):
            wide[p, pl.ds(0, tall), :] = pieces[k, p].astype(F32)
            window = shifted_in(wide[p, pl.ds(skip, n + 8), :], down - skip, right)
            done[k, p] = jnp.where(live, window, 0.0).astype(BF16)

    for part, out in enumerate((theirs_ref, mine_ref)):
        @pl.loop(0, half, unroll=2)
        def _(k):
            cut(part * half + k)
            pltpu.make_async_copy(done.at[part * half + k], out.at[k], store.at[part * half + k]).start()

    for part, out in enumerate((theirs_ref, mine_ref)):
        for k in range(half):
            pltpu.make_async_copy(done.at[part * half + k], out.at[k], store.at[part * half + k]).wait()


def extract(centres, occupied, padded, n):
    count = occupied.shape[2] * centres.shape[2]
    half = count // 2
    shape = jax.ShapeDtypeStruct((half, 2, n, n), BF16)
    smem = pl.BlockSpec(memory_space=pltpu.SMEM)
    return pl.pallas_call(
        functools.partial(extract_kernel, n // 2),
        out_shape=(shape, shape),
        in_specs=[smem, smem, ANY],
        out_specs=(ANY, ANY),
        scratch_shapes=[
            pltpu.VMEM((count, 2, n + 16, n + LANE), BF16),
            pltpu.VMEM((2, n + 24, n + LANE), F32),
            pltpu.SemaphoreType.DMA((count,)),
            pltpu.SemaphoreType.DMA((count,)),
            pltpu.VMEM((count, 2, n, n), BF16),
        ],
        name="extract",
    )(centres, occupied, padded)


def reorder(x, perm_ref, both):
    high, low = split(x)
    if both:
        high = jnp.dot(perm_ref[0], high, preferred_element_type=F32).astype(BF16)
        low = jnp.dot(perm_ref[0], low, preferred_element_type=F32).astype(BF16)
    return jnp.dot(high, perm_ref[1], preferred_element_type=F32) + jnp.dot(low, perm_ref[1], preferred_element_type=F32)


def wave_kernel(
    half, probe_hbm, kern_hbm, mats_hbm, mine_ref, theirs_ref, frames_ref,
    terms_ref, total_ref,
    windows, frames, probe_ref, kern, mats_ref, fixed, grads, total, own_sem, frame_sem, swap_send, swap_recv, term_send, term_recv, term_own, total_sem,
):
    d, r, c = axis_ids()
    n = probe_ref.shape[1]
    steady = [pltpu.make_async_copy(a, b, fixed.at[i]) for i, (a, b) in enumerate([(mats_hbm, mats_ref), (probe_hbm, probe_ref), (kern_hbm, kern)])]
    for copy in steady:
        copy.start()
    partner = (1 - d, r, c)

    def own_copy(k):
        return pltpu.make_async_copy(mine_ref.at[k], windows.at[d, k], own_sem.at[k])

    def frame_copy(k):
        return pltpu.make_async_copy(frames_ref.at[k], frames.at[k], frame_sem.at[k])

    def window_copy(k):
        return remote(theirs_ref.at[k], windows.at[d, k], (swap_send, swap_recv), k, partner)

    def term_copies(k):
        there = terms_ref.at[d * half + k]
        return (
            remote(grads.at[1 - d, k], there, (term_send, term_recv), k, partner),
            pltpu.make_async_copy(grads.at[d, k], there, term_own.at[k]),
        )

    @pl.loop(0, half)
    def _(k):
        own_copy(k).start()

    meet([partner])

    @pl.loop(0, half)
    def _(k):
        window_copy(k).start()
        frame_copy(k).start()

    total[...] = jnp.zeros_like(total)
    forward, inverse = make_transforms(mats_ref)
    for copy in steady:
        copy.wait()

    group = 2

    @pl.loop(0, half // group)
    def _(step):
        ks = [step * group + i for i in range(group)]

        def window(s, k):
            return [windows[s, k, p].astype(F32) for p in range(2)]

        for k in ks:
            own_copy(k).wait()
            frame_copy(k).wait()
            window_copy(k).wait()
        waves = forward([cmul(probe_ref[0], probe_ref[1], *window(0, k)) for k in ks])
        waves = inverse([cmul(fr, fi, kern[0], kern[1]) for fr, fi in waves])
        waves = [(rounded(pr), rounded(pi)) for pr, pi in waves]
        fields = forward([cmul(*wave, *window(1, k)) for wave, k in zip(waves, ks)])
        misfits = [fr * fr + fi * fi - frames[k] for (fr, fi), k in zip(fields, ks)]
        fields = inverse([(m * fr, m * fi) for (fr, fi), m in zip(fields, misfits)], False)
        for k, wave, field in zip(ks, waves, fields):
            gr, gi = conj_mul(*wave, *field)
            grads[1, k, 0] = gr.astype(BF16)
            grads[1, k, 1] = gi.astype(BF16)
        fields = forward([conj_mul(*window(1, k), *field) for k, field in zip(ks, fields)], False)
        fields = inverse([conj_mul(kern[0], kern[1], *field) for field in fields], False)
        fields = [(rounded(xr), rounded(xi)) for xr, xi in fields]
        for k, field in zip(ks, fields):
            gr, gi = conj_mul(probe_ref[0], probe_ref[1], *field)
            grads[0, k, 0] = gr.astype(BF16)
            grads[0, k, 1] = gi.astype(BF16)
            lr, li = conj_mul(*window(0, k), *field)
            total[0] += lr
            total[1] += li
            for copy in term_copies(k):
                copy.start()

    last_copy = pltpu.make_async_copy(total, total_ref, total_sem)
    last_copy.start()

    @pl.loop(0, half)
    def _(k):
        for copy in term_copies(k):
            copy.wait()

    last_copy.wait()


def waves(probe, kern, mats, mine, theirs, frames):
    half, _, n, _ = mine.shape
    dma = pltpu.SemaphoreType.DMA
    return pl.pallas_call(
        functools.partial(wave_kernel, half),
        out_shape=(
            jax.ShapeDtypeStruct((2 * half, 2, n, n), BF16),
            jax.ShapeDtypeStruct((2, n, n), F32),
        ),
        in_specs=[ANY] * 6,
        out_specs=(ANY, ANY),
        scratch_shapes=[
            pltpu.VMEM((2, half, 2, n, n), BF16),
            pltpu.VMEM((half, n, n), F32),
            pltpu.VMEM(probe.shape, F32),
            pltpu.VMEM(kern.shape, F32),
            pltpu.VMEM(mats.shape, BF16),
            dma((3,)),
            pltpu.VMEM((2, half, 2, n, n), BF16),
            pltpu.VMEM((2, n, n), F32),
        ]
        + [dma((half,))] * 7 + [dma(())],
        compiler_params=pltpu.CompilerParams(collective_id=1, has_side_effects=True),
        name="waves",
    )(probe, kern, mats, mine, theirs, frames)


def scatter_kernel(halo, centres, terms_ref, centre_ref, row_ref, side_ref, corner_ref, terms, acc, row_buf, side_buf, corner_buf, load, store):
    _, r, _ = axis_ids()
    count, _, n, _ = terms.shape
    _, _, rows, cols = centre_ref.shape
    slots = centres.shape[2]

    def term_load(p, k):
        return pltpu.make_async_copy(terms_ref.at[k, p], terms.at[k, p], load.at[p, k])

    for p in range(2):
        for k in range(count):
            term_load(p, k).start()
    mine = pl.ds(pl.multiple_of(halo * r, halo), rows)
    far = pl.ds(pl.multiple_of(rows * (1 - r), halo), halo)
    stores = []

    def put(src, dst):
        stores.append(pltpu.make_async_copy(src, dst, store.at[len(stores)]))
        stores[-1].start()

    for p in range(2):
        acc[p] = jnp.zeros(acc.shape[1:], F32)

        @pl.loop(0, count, unroll=8)
        def _(k):
            term_load(p, k).wait()
            row = centres[0, 0, lax.rem(k, slots), 0, k // slots] + halo * (r - 1)
            col = centres[0, 0, lax.rem(k, slots), 1, k // slots]
            top = pl.multiple_of(row // 8 * 8, 8)
            lane = pl.multiple_of(col // LANE * LANE, LANE)
            acc[p, pl.ds(top, n + 8), pl.ds(lane, n + LANE)] += shifted_out(terms[k, p].astype(F32), row - top, col - lane)

        put(acc.at[p, mine, pl.ds(halo, cols)], centre_ref.at[p, 0])
        row_buf[p] = acc[p, far, pl.ds(halo, cols)].astype(BF16)
        put(row_buf.at[p], row_ref.at[p])
        for i, at in enumerate((halo + cols, 0)):
            side_buf[i, p] = acc[p, mine, pl.ds(at, halo)].astype(BF16)
            put(side_buf.at[i, p], side_ref.at[i, p])
            corner_buf[i, p] = acc[p, far, pl.ds(at, halo)].astype(BF16)
            put(corner_buf.at[i, p], corner_ref.at[i, p])
    for copy in stores:
        copy.wait()


def scatter(centres, terms, rows, cols, halo):
    count, _, n, _ = terms.shape
    shapes = [((2, 1, rows, cols), F32), ((2, halo, cols), BF16), ((2, 2, rows, halo), BF16), ((2, 2, halo, halo), BF16)]
    return pl.pallas_call(
        functools.partial(scatter_kernel, halo),
        out_shape=tuple(jax.ShapeDtypeStruct(s, t) for s, t in shapes),
        in_specs=[pl.BlockSpec(memory_space=pltpu.SMEM), ANY],
        out_specs=(ANY,) * 4,
        scratch_shapes=[
            pltpu.VMEM(terms.shape, BF16),
            pltpu.VMEM((2, rows + halo + 8, cols + 2 * halo), F32),
        ]
        + [pltpu.VMEM(s, t) for s, t in shapes[1:]]
        + [pltpu.SemaphoreType.DMA((2, count)), pltpu.SemaphoreType.DMA((12,))],
        name="scatter",
    )(centres, terms)


def x_peer(q):
    d, _, c = axis_ids()
    return (d, q // 2, c // 2 * 2 + lax.rem(q, 2))


def y_peer(q):
    d, r, c = axis_ids()
    return (d, r, c // 8 * 8 + q * 2 + lax.rem(c, 2))


def z_peer(q):
    d, r, c = axis_ids()
    return (d, r, q * 8 + lax.rem(c, 8))


def return_kernel(row_ref, side_ref, corner_ref, total_ref, row_out, side_out, corner_out, probe_out, keep_ref, got_ref, buf, ys_in, y_sum, zs_in, x_in, z_all, local, strips, ys, zs, xs, zg, yg, give):
    d, r, c = axis_ids()
    my_x = r * 2 + lax.rem(c, 2)
    my_y, my_z = lax.rem(c // 2, 4), c // 8
    peers = neighbours()

    def others(me):
        return [lax.rem(me + t, 4) for t in range(1, 4)]

    mid = keep_ref.shape[1]

    def rows_of(depth):
        return total_ref.at[:, pl.ds(pl.multiple_of(depth * mid, 8), mid)]

    load = pltpu.make_async_copy(rows_of(d), keep_ref, local.at[0])
    load.start()
    partner = (1 - d, r, c)
    meet([partner] + peers + [y_peer(q) for q in others(my_y)] + [z_peer(q) for q in others(my_z)])
    other = pltpu.make_async_remote_copy(rows_of(1 - d), got_ref, give[0].at[0], give[1].at[0], device_id=partner, device_id_type=MESH)
    other.start()
    wide = row_ref.shape[-1] // 2
    groups = [[] for _ in range(4)]
    for p in range(2):
        for i in range(2):
            part = (p, slice(None), pl.ds(i * wide, wide))
            groups[2 * p + i].append((row_ref.at[part], row_out.at[part], peers[0]))
            groups[2 * p + i].append((side_ref.at[i, p], side_out.at[i, p], peers[1 + i]))
            groups[2 * p + i].append((corner_ref.at[i, p], corner_out.at[i, p], peers[3 + i]))
    copies = []

    def launch(chosen):
        for s, t, peer in [m for g in chosen for m in groups[g]]:
            copies.append(remote(s, t, strips, len(copies), peer))
            copies[-1].start()

    launch(ORDER[0])
    load.wait()
    other.wait()
    half_rows, n = keep_ref.shape[1:]
    at = 0
    for p in range(2):
        for t in range(half_rows // 8):
            for h in range(n // LANE):
                place = (p, pl.ds(8 * t, 8), pl.ds(LANE * h, LANE))
                buf[at] = keep_ref[place] + got_ref[place]
                at += 1

    def quarter(ref, q):
        size = ref.shape[0] // 4
        return ref.at[pl.ds(q * size, size)]

    sent = []

    def send(src, dst, sems, q, me, peer):
        copy = pltpu.make_async_remote_copy(src, dst, sems[0].at[q], sems[1].at[me], device_id=peer, device_id_type=MESH)
        copy.start()
        sent.append(copy)

    def receive(dst, sems, q, peer):
        pltpu.make_async_remote_copy(dst, dst, sems[0].at[q], sems[1].at[q], device_id=peer, device_id_type=MESH).wait_recv()

    for q in others(my_y):
        send(quarter(buf, q), ys_in.at[my_y], ys, q, my_y, y_peer(q))
    launch(ORDER[1])
    part = quarter(buf, my_y)[...]
    for q in others(my_y):
        receive(ys_in.at[q], ys, q, y_peer(q))
        part = part + ys_in[q]
    y_sum[...] = part
    for q in others(my_z):
        send(quarter(y_sum, q), zs_in.at[my_z], zs, q, my_z, z_peer(q))
    launch(ORDER[2])
    part = quarter(y_sum, my_z)[...]
    for q in others(my_z):
        receive(zs_in.at[q], zs, q, z_peer(q))
        part = part + zs_in[q]
    x_in[my_x] = part
    for q in others(my_x):
        send(x_in.at[my_x], x_in.at[my_x], xs, q, my_x, x_peer(q))
    launch(ORDER[3])
    for q in others(my_x):
        receive(x_in.at[q], xs, q, x_peer(q))
    z_all[my_z] = (x_in[0] + x_in[1]) + (x_in[2] + x_in[3])
    for q in others(my_z):
        send(z_all.at[my_z], z_all.at[my_z], zg, q, my_z, z_peer(q))
    launch(ORDER[4])
    for q in others(my_z):
        receive(z_all.at[q], zg, q, z_peer(q))
    own = pltpu.make_async_copy(z_all, probe_out.at[my_y], local.at[1])
    own.start()
    for q in others(my_y):
        send(z_all, probe_out.at[my_y], yg, q, my_y, y_peer(q))
    launch(ORDER[5])
    for q in others(my_y):
        receive(probe_out.at[q], yg, q, y_peer(q))
    own.wait()
    for copy in sent:
        copy.wait_send()
    for copy in copies:
        copy.wait()


def send_back(row, side, corner, total):
    _, n, _ = total.shape
    share = n * n // (64 * 8 * LANE)
    dma = lambda n: [pltpu.SemaphoreType.DMA((n,)), pltpu.SemaphoreType.DMA((n,))]
    chunk = lambda *lead: pltpu.VMEM(lead + (8, LANE), F32)
    return pl.pallas_call(
        return_kernel_flat,
        out_shape=tuple(jax.ShapeDtypeStruct(a.shape, a.dtype) for a in (row, side, corner)) + (jax.ShapeDtypeStruct((4, 4, 4 * share, 8, LANE), F32),),
        in_specs=[ANY] * 4,
        out_specs=(ANY,) * 4,
        scratch_shapes=[
            pltpu.VMEM((2, n // 2, n), F32),
            pltpu.VMEM((2, n // 2, n), F32),
            chunk(64 * share),
            chunk(4, 16 * share),
            chunk(16 * share),
            chunk(4, 4 * share),
            chunk(4, 4 * share),
            chunk(4, 4 * share),
            pltpu.SemaphoreType.DMA((2,)),
        ]
        + dma(12) + dma(4) * 5 + dma(1),
        compiler_params=pltpu.CompilerParams(collective_id=3, has_side_effects=True),
        name=NAME,
    )(row, side, corner, total)


def return_kernel_flat(*refs):
    sems = refs[17:]
    return_kernel(*refs[:17], *[sems[i : i + 2] for i in range(0, 14, 2)])


def fold_kernel(halo, centre_ref, row_hbm, side_hbm, corner_hbm, chunks_hbm, out_ref, probe_out, sides, middle, row_ref, side_ref, corner_ref, chunks_ref, probe_ref, load, extra, store):
    _, r, _ = axis_ids()
    _, _, rows, cols = out_ref.shape
    edge = pl.ds(pl.multiple_of((rows - halo) * (1 - r), halo), halo)
    inner = pl.ds(halo, cols - 2 * halo)
    strips = [(row_hbm, row_ref), (side_hbm, side_ref), (corner_hbm, corner_ref), (chunks_hbm, chunks_ref)]
    places = []
    for p in range(2):
        places.append((out_ref.at[p, 0, edge, inner], middle.at[p]))
        for i in range(2):
            places.append((out_ref.at[p, 0, :, pl.ds(i * (cols - halo), halo)], sides.at[i, p]))
    brought = [pltpu.make_async_copy(a, b, extra.at[j]) for j, (a, b) in enumerate(strips)]
    loads = [pltpu.make_async_copy(a, b, load.at[j]) for j, (a, b) in enumerate(places)]
    stores = [pltpu.make_async_copy(b, a, store.at[j]) for j, (a, b) in enumerate(places)]
    stores.append(pltpu.make_async_copy(probe_ref, probe_out, store.at[len(places)]))
    brought[0].start()
    loads[0].start()
    brought[1].start()
    brought[2].start()
    for copy in loads[1:]:
        copy.start()
    brought[3].start()
    for copy in brought[:3]:
        copy.wait()
    for p in range(2):
        loads[3 * p].wait()
        middle[p] += row_ref[p, :, inner].astype(F32)
        stores[3 * p].start()
        for i in range(2):
            loads[3 * p + 1 + i].wait()
            sides[i, p] += side_ref[i, p].astype(F32)
            sides[i, p, edge, :] += row_ref[p, :, pl.ds(i * (cols - halo), halo)].astype(F32) + corner_ref[i, p].astype(F32)
            stores[3 * p + 1 + i].start()
    brought[3].wait()
    at = 0
    _, half_rows, n = probe_ref.shape
    for p in range(2):
        for t in range(half_rows // 8):
            for h in range(n // LANE):
                probe_ref[p, pl.ds(8 * t, 8), pl.ds(LANE * h, LANE)] = chunks_ref[at // 16, at // 4 % 4, at % 4]
                at += 1
    stores[-1].start()
    for copy in stores:
        copy.wait()


def fold(centre, row, side, corner, chunks, n):
    halo = row.shape[1]
    _, _, rows, cols = centre.shape
    return pl.pallas_call(
        functools.partial(fold_kernel, halo),
        out_shape=(jax.ShapeDtypeStruct(centre.shape, F32), jax.ShapeDtypeStruct((2, n // 2, n), F32)),
        in_specs=[ANY] * 5,
        out_specs=(ANY, ANY),
        scratch_shapes=[
            pltpu.VMEM((2, 2, rows, halo), F32),
            pltpu.VMEM((2, halo, cols - 2 * halo), F32),
        ]
        + [pltpu.VMEM(a.shape, a.dtype) for a in (row, side, corner, chunks)]
        + [pltpu.VMEM((2, n // 2, n), F32)]
        + [pltpu.SemaphoreType.DMA((6,)), pltpu.SemaphoreType.DMA((4,)), pltpu.SemaphoreType.DMA((7,))],
        input_output_aliases={0: 0},
        name="fold",
    )(centre, row, side, corner, chunks)


def shards(probe, object_re, object_im, phases, centres, occupied, measured):
    n = probe.shape[1]
    _, rows, cols = object_re.shape
    mats, perm = (jnp.asarray(x) for x in constants(n))
    centres = jnp.transpose(centres, (0, 1, 3, 4, 2))
    padded, kern, frames = exchange_halo(object_re, object_im, phases, perm, measured, n // 2)
    mine, theirs = extract(centres, occupied, padded, n)
    terms, total = waves(probe, kern, mats, mine, theirs, frames)
    centre, row, side, corner = scatter(centres, terms, rows, cols, n // 2)
    row, side, corner, chunks = send_back(row, side, corner, total)
    return fold(centre, row, side, corner, chunks, n)


def solution(mesh):
    in_specs = (
        P(),
        P("depth", "row", "col"),
        P("depth", "row", "col"),
        P(),
        P("row", "col", None, None, None),
        P("row", "col", None),
        P("row", "col", None, None, None, None),
    )
    out_specs = (P(None, "depth", "row", "col"), P(None, "depth", None))
    return jax.shard_map(shards, mesh=mesh, in_specs=in_specs, out_specs=out_specs, check_vma=False)
```
